512 devices in a mesh: pw: 32 (over y_lo, z), band: 16 (over y_hi, x, core).
Axes of the slice: x: 4, y: 4 (y_hi: 2, y_lo: 2; y = y_hi * 2 + y_lo), z: 16, core: 2. Of those that a mesh axis runs over, the one named last changes fastest.
Arguments:
- psi_occ: bfloat16 [2, 256, 49152], P(None, 'band', 'pw'), may hold values from -0.2890625 to 0.2890625
- psi_high: bfloat16 [2, 4096, 49152], P(None, 'band', 'pw'), may hold values from -0.2890625 to 0.2890625
- miller: int32 [3, 49152], P(None, 'pw'), may hold values from -24 to 24
- recip: float32 [3, 3], replicated, may hold values from -0.1 to 0.1
- kfrac: float32 [3], replicated, may hold values from -0.5 to 0.5
- positions: float32 [48, 3], replicated, may hold values from 0 to 20
- atom_type: int32 [48], replicated, may hold values from 0 to 2
- proj_atom: int32 [192], replicated, may hold values from 0 to 47
- widths: float32 [3], replicated, may hold values from 0.2 to 2
- dion: float32 [3], replicated, may hold values from 0.03 to 0.15
Outputs:
- dipole: float32 [3, 2, 256, 4096], P(None, None, 'pw', 'band')
The draws below stay inside these ranges and needn't reach their ends.
All inputs are finite; a program needn't handle non-finite values.
Results may differ from the reference program's by a relative error of at most 0.0046.
Values may be sent and summed in bfloat16 or wider, within the bound.
A program may use at most 64 MiB of HBM per device.

```python
import math
import jax
import jax.numpy as jnp
from jax import lax

NPW = 49152
NOCC = 256
NHIGH = 4096
NPROJ = 192
NTYPE = 3
NATOM = 48
N_PW = 32


def place_ends(result, stream_key, smallest, top_value):
    spot = [jax.random.randint(jax.random.fold_in(stream_key, axis), (), 0, length) for axis, length in enumerate(result.shape)]
    widest = result.shape.index(max(result.shape))
    beside = spot[:widest] + [(spot[widest] + 1) % result.shape[widest]] + spot[widest + 1:]
    return result.at[tuple(spot)].set(smallest).at[tuple(beside)].set(top_value)


def block_levels(stream_key, shape, shards, least, high):
    loudness, own = 1.0, jax.random.fold_in(stream_key, 6)
    for axis_at, blocks in shards:
        steps = jnp.exp(jax.random.uniform(jax.random.fold_in(own, axis_at), (blocks,), jnp.float32, least / len(shards), high / len(shards)))
        loudness = loudness * jnp.repeat(steps, shape[axis_at] // blocks).reshape([-1 if axis == axis_at else 1 for axis in range(len(shape))])
    return loudness


def centred(rng, shape, width, most, pieces=(), kind=jnp.bfloat16):
    drawn = jax.random.normal(rng, shape, jnp.float32) * width
    if len(pieces) > 0:
        drawn = block_levels(rng, shape, pieces, -0.22, 0.18) * drawn
    return jnp.clip(drawn, min=-most, max=most).astype(kind)


def setup_inputs(seed: int = 0) -> dict:
    seeds = jax.random.split(jax.random.key(seed), 11)
    psi_occ = centred(seeds[0], (2, NOCC, NPW), 0.04, 0.2890625, ((1, 16), (2, 32)))
    psi_high = centred(seeds[1], (2, NHIGH, NPW), 0.04, 0.2890625, ((1, 16), (2, 32)))
    miller = place_ends(jax.random.randint(seeds[2], (3, NPW), -24, 25), jax.random.fold_in(seeds[2], 1), -24, 24).astype(jnp.int32)
    recip = jnp.clip(jax.random.uniform(seeds[3], (3, 3), jnp.float32, -0.1, 0.1), -0.1, 0.1)
    kfrac = jnp.clip(jax.random.uniform(seeds[4], (3,), jnp.float32, -0.5, 0.5), -0.5, 0.5)
    positions = jnp.clip(jax.random.uniform(seeds[5], (NATOM, 3), jnp.float32, 0.0, 20.0), 0.0, 20.0)
    atom_type = place_ends(jax.random.randint(seeds[6], (NATOM,), 0, NTYPE), jax.random.fold_in(seeds[6], 1), 0, NTYPE - 1).astype(jnp.int32)
    proj_atom = place_ends(jax.random.randint(seeds[7], (NPROJ,), 0, NATOM), jax.random.fold_in(seeds[7], 1), 0, NATOM - 1).astype(jnp.int32)
    widths = jnp.clip(jnp.exp(jax.random.uniform(seeds[8], (NTYPE,), jnp.float32, math.log(0.2), math.log(2.0))), 0.2, 2.0)
    dion = jnp.clip(jnp.exp(jax.random.uniform(seeds[9], (NTYPE,), jnp.float32, math.log(0.03), math.log(0.15))), 0.03, 0.15)
    return {"psi_occ": psi_occ, "psi_high": psi_high, "miller": miller, "recip": recip, "kfrac": kfrac, "positions": positions, "atom_type": atom_type, "proj_atom": proj_atom, "widths": widths, "dion": dion}


def wave_vectors(miller, recip, kfrac):
    shifted = miller.astype(jnp.float32) + kfrac[:, None]
    return shifted[0][None, :] * recip[0][:, None] + shifted[1][None, :] * recip[1][:, None] + shifted[2][None, :] * recip[2][:, None]


def build_projectors(wavevec, centers, spread, channel):
    square = jnp.sum(wavevec * wavevec, axis=0)
    envelope = jnp.exp(-0.5 * spread[:, None] * square[None, :])
    selectors = [(channel == channel_id).astype(jnp.float32)[:, None] for channel_id in range(4)]
    angular = selectors[0] + selectors[1] * wavevec[0][None, :] + selectors[2] * wavevec[1][None, :] + selectors[3] * wavevec[2][None, :]
    phases = centers[:, 0:1] * wavevec[0][None, :] + centers[:, 1:2] * wavevec[1][None, :] + centers[:, 2:3] * wavevec[2][None, :]
    cosine_part = jnp.cos(phases)
    sine_part = jnp.sin(phases)
    radial = envelope * angular
    stacked_kinds = [jnp.concatenate([radial * cosine_part, -radial * sine_part], axis=1)]
    for direction in range(3):
        factor = envelope * (selectors[direction + 1] - spread[:, None] * wavevec[direction][None, :] * angular)
        stacked_kinds.append(jnp.concatenate([factor * sine_part, factor * cosine_part], axis=1))
    return jnp.stack(stacked_kinds).astype(jnp.bfloat16)


def pair_forms(values):
    return jnp.stack([jnp.concatenate([values[0], values[1]], axis=-1), jnp.concatenate([values[1], -values[0]], axis=-1)])


def swapped(values):
    return jnp.stack([values[:, 1], -values[:, 0]], axis=1)


def nonlocal_terms(occ_weighted, high_coef):
    hp = lax.Precision.HIGHEST
    real_part = jnp.einsum('cmi,acin->amn', occ_weighted[0], high_coef[1:], precision=hp) - jnp.einsum('acmi,cin->amn', occ_weighted[1:], high_coef[0], precision=hp)
    other = swapped(high_coef)
    imag_part = jnp.einsum('cmi,acin->amn', occ_weighted[0], other[1:], precision=hp) - jnp.einsum('acmi,cin->amn', occ_weighted[1:], other[0], precision=hp)
    return real_part, imag_part


def reference(psi_occ, psi_high, miller, recip, kfrac, positions, atom_type, proj_atom, widths, dion):
    width_block = NPW // N_PW
    kind_of = atom_type[proj_atom]
    centers = positions[proj_atom]
    spread = widths[kind_of]
    strength = dion[kind_of]
    channel = (jnp.arange(NPROJ) % 4).astype(jnp.int32)

    def accumulate(totals, block_id):
        momentum, occ_coef, high_coef = totals
        offset = (block_id * width_block).astype(jnp.int32)
        occ_block = lax.dynamic_slice_in_dim(psi_occ, offset, width_block, 2)
        high_block = lax.dynamic_slice_in_dim(psi_high, offset, width_block, 2)
        miller_block = lax.dynamic_slice_in_dim(miller, offset, width_block, 1)
        wavevec = wave_vectors(miller_block, recip, kfrac)
        projectors = build_projectors(wavevec, centers, spread, channel).astype(jnp.float32)
        high_pair = pair_forms(high_block).astype(jnp.float32)
        occ_cat = jnp.concatenate([occ_block[0], occ_block[1]], axis=-1).astype(jnp.float32)
        parts = []
        for direction in range(3):
            doubled = jnp.concatenate([wavevec[direction], wavevec[direction]])
            scaled = (doubled[None, :] * occ_cat).astype(jnp.bfloat16).astype(jnp.float32)
            parts.append(jnp.einsum('rg,cng->crn', scaled, high_pair))
        momentum = momentum + jnp.stack(parts)
        proj_pair = jnp.stack([projectors, jnp.concatenate([-projectors[:, :, width_block:], projectors[:, :, :width_block]], axis=-1)], axis=1)
        occ_coef = occ_coef + jnp.einsum('kcig,rg->kcri', proj_pair, occ_cat)
        high_coef = high_coef + jnp.einsum('kig,cng->kcin', projectors, high_pair)
        return (momentum, occ_coef, high_coef), None

    start_totals = (jnp.zeros((3, 2, NOCC, NHIGH), jnp.float32), jnp.zeros((4, 2, NOCC, NPROJ), jnp.float32), jnp.zeros((4, 2, NPROJ, NHIGH), jnp.float32))
    totals, _ = lax.scan(accumulate, start_totals, jnp.arange(N_PW, dtype=jnp.int32))
    momentum, occ_coef, high_coef = totals
    occ_weighted = occ_coef * strength[None, None, None, :]
    real_part, imag_part = nonlocal_terms(occ_weighted, high_coef)
    return jnp.stack([momentum[:, 0] - imag_part, momentum[:, 1] + real_part], axis=1)
```

```python
import functools

import jax
import jax.numpy as jnp
from jax import lax
from jax.experimental import pallas as pl
from jax.experimental.pallas import tpu as pltpu
from jax.sharding import PartitionSpec as P

MESH = pl.DeviceIdType.MESH
F32 = jnp.float32
BF16 = jnp.bfloat16
LANES = 512


def projector_table(positions, atom_type, proj_atom, widths, dion):
    hp = lax.Precision.HIGHEST
    atom_hot = (
        proj_atom[:, None] == jnp.arange(positions.shape[0], dtype=jnp.int32)[None, :]
    ).astype(F32)
    type_hot = (atom_type[:, None] == jnp.arange(widths.shape[0], dtype=jnp.int32)[None, :]).astype(F32)
    per_type = jnp.stack([widths, dion], axis=1)
    per_atom = jnp.concatenate([positions, jnp.dot(type_hot, per_type, precision=hp)], axis=1)
    return jnp.dot(atom_hot, per_atom, precision=hp)


def sin_cos(angle):
    turns = jnp.floor(angle * 0.6366197723675814 + 0.5)
    rest = angle - turns * 1.5703125
    rest = rest - turns * 4.837512969970703125e-4
    rest = rest - turns * 7.54978995489188216e-8
    square = rest * rest
    sine = rest + rest * square * (
        -1.6666654611e-1 + square * (8.3321608736e-3 + square * -1.9515295891e-4)
    )
    cosine = (
        1.0
        - 0.5 * square
        + square * square * (4.166664568298827e-2 + square * (-1.388731625493765e-3 + square * 2.443315711809948e-5))
    )
    quadrant = turns - 4.0 * jnp.floor(turns * 0.25)
    odd = (quadrant == 1.0) | (quadrant == 3.0)
    first = jnp.where(odd, cosine, sine)
    second = jnp.where(odd, sine, cosine)
    sine = jnp.where(quadrant >= 2.0, -first, first)
    cosine = jnp.where((quadrant == 1.0) | (quadrant == 2.0), -second, second)
    return sine, cosine


def dot_t(lhs, rhs):
    return lax.dot_general(lhs, rhs, (((1,), (1,)), ((), ())), preferred_element_type=F32)


def kernel(
    nz,
    nx,
    occ_ref,
    high_ref,
    miller_ref,
    par_ref,
    strength_ref,
    recip_ref,
    kfrac_ref,
    out_ref,
    occ_all,
    wave,
    stage,
    proj,
    occ_a,
    occ_b,
    coef,
    occ_coef,
    occ_tile,
    scaled,
    total,
    ys1,
    yr1,
    oyr,
    us1,
    ur1,
    ds1,
    dr1,
    ys2,
    yr2,
    us2,
    ur2,
    ds2,
    dr2,
    tile_own,
    tiles,
    g_send,
    g_recv,
    y1_send,
    y1_recv,
    oy_send,
    oy_recv,
    u1_send,
    u1_recv,
    d1_send,
    d1_recv,
    y2_send,
    y2_recv,
    u2_send,
    u2_recv,
    d2_send,
    d2_recv,
    t_send,
    t_recv,
):
    p = lax.axis_index("pw")
    b = lax.axis_index("band")
    nband = 4 * nx
    y_lo, z = p // nz, p % nz
    y_hi, x, core = b // (2 * nx), (b // 2) % nx, b % 2
    half = nz // 2
    width = high_ref.shape[2]

    def band_id(yy, xx, cc):
        return yy * (2 * nx) + xx * 2 + cc

    def pw_id(yy, zz):
        return yy * nz + zz

    def put(src, dst, send, recv, pw, band):
        return pltpu.make_async_remote_copy(
            src_ref=src,
            dst_ref=dst,
            send_sem=send,
            recv_sem=recv,
            device_id={"pw": pw, "band": band},
            device_id_type=MESH,
        )

    y_mate = pw_id(1 - y_lo, z)
    z_up = pw_id(y_lo, (z + 1) % nz)
    z_down = pw_id(y_lo, (z + nz - 1) % nz)

    barrier = pltpu.get_barrier_semaphore()
    for pw in (y_mate, z_up, z_down):
        pl.semaphore_signal(barrier, inc=1, device_id={"pw": pw, "band": b}, device_id_type=MESH)
    for step in range(1, nband):
        pl.semaphore_signal(
            barrier, inc=1, device_id={"pw": p, "band": (b + step) % nband}, device_id_type=MESH
        )
    pl.semaphore_wait(barrier, 3 + nband - 1)

    started = []

    def forward(src, block, count, bands):
        for band in bands:
            copy = put(src, occ_all.at[block], g_send.at[count], g_recv.at[block], p, band)
            copy.start()
            started.append(copy)
            count += 1
        return count

    def block_arrived(block):
        put(occ_all.at[block], occ_all.at[block], g_send.at[0], g_recv.at[block], p, b).wait_recv()

    mate_block = band_id(1 - y_hi, x, core)
    x_others = [(x + dx) % nx for dx in range(1, nx)]
    sent = forward(
        occ_ref,
        b,
        0,
        [mate_block] + [band_id(y_hi, xx, core) for xx in x_others] + [band_id(y_hi, x, 1 - core)],
    )
    occ_all[b] = occ_ref[...]

    shifted = [miller_ref[axis : axis + 1, :].astype(F32) + kfrac_ref[axis] for axis in range(3)]
    vectors = [
        shifted[0] * recip_ref[0, axis] + shifted[1] * recip_ref[1, axis] + shifted[2] * recip_ref[2, axis]
        for axis in range(3)
    ]
    for axis in range(3):
        wave[axis] = jnp.broadcast_to(vectors[axis], (8, width))
    wave[3] = jnp.broadcast_to(
        vectors[0] * vectors[0] + vectors[1] * vectors[1] + vectors[2] * vectors[2], (8, width)
    )
    nown = occ_ref.shape[1]
    occ_a[...] = jnp.zeros_like(occ_a)
    occ_b[...] = jnp.zeros_like(occ_b)
    occ_a[0:nown, :] = occ_ref[0]
    occ_a[nown : 2 * nown, :] = occ_ref[1]
    occ_b[0:nown, :] = occ_ref[1]
    occ_b[nown : 2 * nown, :] = -occ_ref[0]

    channel = lax.broadcasted_iota(jnp.int32, (8, LANES), 0) % 4
    selectors = [(channel == value).astype(F32) for value in range(4)]
    pieces = width // LANES

    def place(part, kind, value):
        for piece in range(LANES // 128):
            stage[part, piece, pl.ds(kind, 8, stride=4), :] = value[:, 128 * piece : 128 * piece + 128]

    def build(index, carry):
        block = index // pieces
        columns = pl.ds(pl.multiple_of((index % pieces) * LANES, LANES), LANES)
        table = par_ref[pl.ds(pl.multiple_of(block * 8, 8), 8), :]
        k = [wave[axis, :, columns] for axis in range(3)]
        square = wave[3, :, columns]
        spread = table[:, 3:4]
        envelope = jnp.exp(-0.5 * spread * square)
        angular = selectors[0] + selectors[1] * k[0] + selectors[2] * k[1] + selectors[3] * k[2]
        sine, cosine = sin_cos(table[:, 0:1] * k[0] + table[:, 1:2] * k[1] + table[:, 2:3] * k[2])
        radial = envelope * angular
        place(0, 0, radial * cosine)
        place(1, 0, -radial * sine)
        for axis in range(3):
            factor = envelope * (selectors[axis + 1] - spread * k[axis] * angular)
            place(0, axis + 1, factor * sine)
            place(1, axis + 1, factor * cosine)
        rows = pl.ds(pl.multiple_of(block * 32, 32), 32)
        for part in range(2):
            pieces_of = [stage[part, piece] for piece in range(LANES // 128)]
            proj[part, rows, columns] = jnp.concatenate(pieces_of, axis=1).astype(BF16)
        return carry

    lax.fori_loop(0, (par_ref.shape[0] // 8) * pieces, build, 0)

    block_arrived(mate_block)
    sent = forward(
        occ_all.at[mate_block],
        mate_block,
        sent,
        [band_id(y_hi, xx, core) for xx in x_others] + [band_id(y_hi, x, 1 - core)],
    )

    coef[...] = jnp.zeros_like(coef)
    occ_coef[...] = jnp.zeros_like(occ_coef)

    def project(index, carry):
        columns = pl.ds(pl.multiple_of(index * 256, 256), 256)
        real, imag = proj[0, :, columns], proj[1, :, columns]
        high_r, high_i = high_ref[0, :, columns], high_ref[1, :, columns]
        occ_coef[...] += dot_t(real, occ_a[:, columns]) + dot_t(imag, occ_b[:, columns])
        coef[0] += dot_t(real, high_r) + dot_t(imag, high_i)
        coef[1] += dot_t(real, high_i) - dot_t(imag, high_r)
        return carry

    lax.fori_loop(0, width // 256, project, 0)

    npw = 2 * nz
    for owner in range(npw):
        rows = occ_coef[24 * owner : 24 * owner + 24, :] * strength_ref[24 * owner : 24 * owner + 24, :]
        occ_tile[owner] = (
            rows[0:8] + pltpu.roll(rows[8:16], 32, 1) + pltpu.roll(rows[16:24], 64, 1)
        )

    def chunk1(owner):
        return coef[:, pl.ds(pl.multiple_of(owner * 24, 8), 24), :].reshape(48, 256)

    def chunk2(owner):
        return total[:, :, pl.ds(pl.multiple_of(owner * 8, 8), 8), :].reshape(48, 256)

    def up_dest(step):
        return (z + half - step + nz) % nz

    def down_dest(step):
        return (z + half + 1 + step) % nz

    def mate_sends(chunk, ys, yr, send, recv):
        copies = []
        for step in range(half):
            ys[step, 0] = chunk(pw_id(1 - y_lo, up_dest(step))).astype(BF16)
            ys[step, 1] = chunk(pw_id(1 - y_lo, down_dest(step))).astype(BF16)
            copy = put(ys.at[step], yr.at[step], send.at[step], recv.at[step], y_mate, b)
            copy.start()
            copies.append(copy)
        return copies

    tile_copy = put(
        occ_tile.at[pl.ds((1 - y_lo) * nz, nz)], oyr, oy_send.at[0], oy_recv.at[0], y_mate, b
    )
    tile_copy.start()
    mates1 = mate_sends(chunk1, ys1, yr1, y1_send, y1_recv)

    def occ_sum(dest):
        tile = occ_tile[pw_id(y_lo, dest)] + oyr[dest]
        return jnp.concatenate([tile, jnp.zeros_like(tile)], axis=1)

    for yy in (y_hi, 1 - y_hi):
        for xx in x_others:
            block = band_id(yy, xx, core)
            block_arrived(block)
            sent = forward(occ_all.at[block], block, sent, [band_id(y_hi, x, 1 - core)])
    tile_copy.wait_recv()
    total[...] = jnp.zeros_like(total)

    rings = []

    def ring_step(step, chunk, yr, mates, us, ur, ds, dr, u_send, u_recv, d_send, d_recv, tail):
        mates[step].wait_recv()
        if step > 0:
            rings_up[step - 1].wait_recv()
        dest = up_dest(step)
        value = chunk(pw_id(y_lo, dest)) + yr[step, 0].astype(F32)
        if step > 0:
            value = value + ur[step - 1, 0:48, :]
        us[step, 0:48, :] = value
        if tail:
            extra = occ_sum(dest)
            if step > 0:
                extra = extra + ur[step - 1, 48:56, :]
            us[step, 48:56, :] = extra
        copy = put(us.at[step], ur.at[step], u_send.at[step], u_recv.at[step], z_up, b)
        copy.start()
        rings_up.append(copy)
        if step < half - 1:
            if step > 0:
                rings_down[step - 1].wait_recv()
            dest = down_dest(step)
            value = chunk(pw_id(y_lo, dest)) + yr[step, 1].astype(F32)
            if step > 0:
                value = value + dr[step - 1, 0:48, :]
            ds[step, 0:48, :] = value
            if tail:
                extra = occ_sum(dest)
                if step > 0:
                    extra = extra + dr[step - 1, 48:56, :]
                ds[step, 48:56, :] = extra
            copy = put(ds.at[step], dr.at[step], d_send.at[step], d_recv.at[step], z_down, b)
            copy.start()
            rings_down.append(copy)

    def ring_end(chunk, yr, ur, dr):
        rings_up[half - 1].wait_recv()
        rings_down[half - 2].wait_recv()
        value = chunk(pw_id(y_lo, z)) + yr[half - 1, 1].astype(F32)
        return value + ur[half - 1, 0:48, :] + dr[half - 2, 0:48, :]

    nocc = total.shape[2]

    def momentum_piece(index):
        columns = pl.ds(pl.multiple_of(index * 256, 256), 256)
        for part in range(2):
            values = occ_all[:, part, :, columns].reshape(nocc, 256).astype(F32)
            for axis in range(3):
                vector = wave[axis, 0:1, columns]
                scaled[part, axis * nocc : (axis + 1) * nocc, :] = (values * vector).astype(BF16)
        real, imag = scaled[0], scaled[1]
        high_r, high_i = high_ref[0, :, columns], high_ref[1, :, columns]
        total[0] += (dot_t(real, high_r) + dot_t(imag, high_i)).reshape(3, nocc, 256)
        total[1] += (dot_t(real, high_i) - dot_t(imag, high_r)).reshape(3, nocc, 256)

    rings_up, rings_down = [], []
    ring_refs = (us1, ur1, ds1, dr1, u1_send, u1_recv, d1_send, d1_recv)
    ring_step(0, chunk1, yr1, mates1, *ring_refs, True)
    for xx in [x] + x_others:
        for yy in range(2):
            block_arrived(band_id(yy, xx, 1 - core))
    for step in range(1, half):
        ring_step(step, chunk1, yr1, mates1, *ring_refs, True)
        if step - 1 < width // 256:
            momentum_piece(step - 1)
    for index in range(half - 1, width // 256):
        momentum_piece(index)
    high_sum = ring_end(chunk1, yr1, ur1, dr1)
    tile_own[...] = (
        occ_tile[p] + oyr[z] + ur1[half - 1, 48:56, 0:128] + dr1[half - 2, 48:56, 0:128]
    )
    rings1 = rings_up + rings_down

    tile_copies = []
    for step in range(1, nband):
        copy = put(
            tile_own, tiles.at[b], t_send.at[step - 1], t_recv.at[b], p, (b + step) % nband
        )
        copy.start()
        tile_copies.append(copy)
    tiles[b] = tile_own[...]
    high_hi = high_sum.astype(BF16)
    high_lo = (high_sum - high_hi.astype(F32)).astype(BF16)
    rhs = jnp.concatenate([high_hi, high_lo, high_hi], axis=0)
    for step in range(1, nband):
        block = (b + step) % nband
        put(tile_own, tiles.at[block], t_send.at[0], t_recv.at[block], p, b).wait_recv()

    lane_block = lax.broadcasted_iota(jnp.int32, (8, 128), 1) // 16
    occ_sums = []
    for part in range(2):
        groups = []
        for group in range(3):
            halves = []
            for side in range(nband // 8):
                value = jnp.zeros((8, 128), F32)
                for place in range(8):
                    shift = (16 * place - 32 * group - 16 * part) % 128
                    tile = tiles[8 * side + place]
                    if shift:
                        tile = pltpu.roll(tile, shift, 1)
                    value = jnp.where(lane_block == place, tile, value)
                halves.append(value)
            groups.append(jnp.concatenate(halves, axis=1))
        occ_sums.append(jnp.concatenate(groups, axis=0))
    kind = lax.broadcasted_iota(jnp.int32, (24, 256), 0) % 4
    for axis in range(3):
        mixed = []
        for part in range(2):
            value = occ_sums[part]
            lower = pltpu.roll(value, axis + 1, 0)
            upper = pltpu.roll(value, 24 - (axis + 1), 0)
            mixed.append(
                jnp.where(kind == axis + 1, lower, jnp.where(kind == 0, -upper, jnp.zeros_like(value)))
            )
        for part in range(2):
            if part == 0:
                left = jnp.concatenate([mixed[1], -mixed[0]], axis=0)
            else:
                left = jnp.concatenate([mixed[0], mixed[1]], axis=0)
            left_hi = left.astype(BF16)
            left_lo = (left - left_hi.astype(F32)).astype(BF16)
            lhs = jnp.concatenate([left_hi, left_hi, left_lo], axis=0)
            total[part, axis] += lax.dot_general(
                lhs, rhs, (((0,), (0,)), ((), ())), preferred_element_type=F32
            )

    mates2 = mate_sends(chunk2, ys2, yr2, y2_send, y2_recv)
    rings_up, rings_down = [], []
    ring_refs = (us2, ur2, ds2, dr2, u2_send, u2_recv, d2_send, d2_recv)
    for step in range(half):
        ring_step(step, chunk2, yr2, mates2, *ring_refs, False)
    result = ring_end(chunk2, yr2, ur2, dr2).reshape(2, 3, 8, 256)
    for axis in range(3):
        for part in range(2):
            out_ref[axis, part] = result[part, axis]

    for copy in started + [tile_copy] + mates1 + rings1 + tile_copies + mates2 + rings_up + rings_down:
        copy.wait_send()


def on_device(
    nz, nx, psi_occ, psi_high, miller, recip, kfrac, positions, atom_type, proj_atom, widths, dion
):
    nproj = proj_atom.shape[0]
    nown, nhigh, width = psi_occ.shape[1], psi_high.shape[1], psi_high.shape[2]
    npw, nband, half = 2 * nz, 4 * nx, nz // 2
    nocc = nown * nband
    table = projector_table(positions, atom_type, proj_atom, widths, dion)
    strength = jnp.broadcast_to(jnp.repeat(table[:, 4:5], 4, axis=0), (4 * nproj, 128))
    vmem, smem = pltpu.VMEM, pltpu.SMEM
    dma = pltpu.SemaphoreType.DMA
    out = pl.pallas_call(
        functools.partial(kernel, nz, nx),
        out_shape=jax.ShapeDtypeStruct((3, 2, nocc // npw, nhigh), F32),
        in_specs=[pl.BlockSpec(memory_space=vmem)] * 5 + [pl.BlockSpec(memory_space=smem)] * 2,
        out_specs=pl.BlockSpec(memory_space=vmem),
        scratch_shapes=[
            vmem((nband, 2, nown, width), BF16),
            vmem((4, 8, width), F32),
            vmem((2, LANES // 128, 32, 128), F32),
            vmem((2, 4 * nproj, width), BF16),
            vmem((128, width), BF16),
            vmem((128, width), BF16),
            vmem((2, 4 * nproj, nhigh), F32),
            vmem((4 * nproj, 128), F32),
            vmem((npw, 8, 128), F32),
            vmem((2, 3 * nocc, 256), BF16),
            vmem((2, 3, nocc, nhigh), F32),
            vmem((half, 2, 48, nhigh), BF16),
            vmem((half, 2, 48, nhigh), BF16),
            vmem((nz, 8, 128), F32),
            vmem((half, 56, nhigh), F32),
            vmem((half, 56, nhigh), F32),
            vmem((half - 1, 56, nhigh), F32),
            vmem((half - 1, 56, nhigh), F32),
            vmem((half, 2, 48, nhigh), BF16),
            vmem((half, 2, 48, nhigh), BF16),
            vmem((half, 48, nhigh), F32),
            vmem((half, 48, nhigh), F32),
            vmem((half - 1, 48, nhigh), F32),
            vmem((half - 1, 48, nhigh), F32),
            vmem((8, 128), F32),
            vmem((nband, 8, 128), F32),
            dma((nband - 1,)),
            dma((nband,)),
            dma((half,)),
            dma((half,)),
            dma((1,)),
            dma((1,)),
            dma((half,)),
            dma((half,)),
            dma((half - 1,)),
            dma((half - 1,)),
            dma((half,)),
            dma((half,)),
            dma((half,)),
            dma((half,)),
            dma((half - 1,)),
            dma((half - 1,)),
            dma((nband - 1,)),
            dma((nband,)),
        ],
        compiler_params=pltpu.CompilerParams(
            collective_id=0, has_side_effects=True, vmem_limit_bytes=52 * 1024 * 1024
        ),
    )(psi_occ, psi_high, miller, table, strength, recip, kfrac)
    return out


def solution(mesh):
    nz = mesh.shape["pw"] // 2
    nx = mesh.shape["band"] // 4
    placed = (
        P(None, "band", "pw"),
        P(None, "band", "pw"),
        P(None, "pw"),
        P(),
        P(),
        P(),
        P(),
        P(),
        P(),
        P(),
    )
    return jax.shard_map(
        functools.partial(on_device, nz, nx),
        mesh=mesh,
        in_specs=placed,
        out_specs=P(None, None, "pw", "band"),
        check_vma=False,
    )
```

```python
import functools

import jax
import jax.numpy as jnp
from jax import lax
from jax.experimental import pallas as pl
from jax.experimental.pallas import tpu as pltpu
from jax.sharding import PartitionSpec as P

MESH = pl.DeviceIdType.MESH
F32 = jnp.float32
BF16 = jnp.bfloat16
LANES = 512
MOVES = [(8, 4), (-7, -3), (7, 3), (-6, -2), (6, 2), (-5, -1), (5, 1)]
RELAYS = [4, -4]
DIRECT = [3, -3, 2, -2, 1, -1]
ORDER = [offset for offset, _ in MOVES] + RELAYS + DIRECT + [0]


def projector_table(positions, atom_type, proj_atom, widths, dion):
    hp = lax.Precision.HIGHEST
    atom_hot = (
        proj_atom[:, None] == jnp.arange(positions.shape[0], dtype=jnp.int32)[None, :]
    ).astype(F32)
    type_hot = (atom_type[:, None] == jnp.arange(widths.shape[0], dtype=jnp.int32)[None, :]).astype(F32)
    per_type = jnp.stack([widths, dion], axis=1)
    per_atom = jnp.concatenate([positions, jnp.dot(type_hot, per_type, precision=hp)], axis=1)
    return jnp.dot(atom_hot, per_atom, precision=hp)


def sin_cos(angle):
    turns = jnp.floor(angle * 0.6366197723675814 + 0.5)
    rest = angle - turns * 1.5703125
    rest = rest - turns * 4.837512969970703125e-4
    rest = rest - turns * 7.54978995489188216e-8
    square = rest * rest
    sine = rest + rest * square * (
        -1.6666654611e-1 + square * (8.3321608736e-3 + square * -1.9515295891e-4)
    )
    cosine = (
        1.0
        - 0.5 * square
        + square * square * (4.166664568298827e-2 + square * (-1.388731625493765e-3 + square * 2.443315711809948e-5))
    )
    quadrant = turns - 4.0 * jnp.floor(turns * 0.25)
    odd = (quadrant == 1.0) | (quadrant == 3.0)
    first = jnp.where(odd, cosine, sine)
    second = jnp.where(odd, sine, cosine)
    sine = jnp.where(quadrant >= 2.0, -first, first)
    cosine = jnp.where((quadrant == 1.0) | (quadrant == 2.0), -second, second)
    return sine, cosine


def dot_t(lhs, rhs):
    return lax.dot_general(lhs, rhs, (((1,), (1,)), ((), ())), preferred_element_type=F32)


def kernel(
    nz,
    nx,
    occ_ref,
    high_ref,
    miller_ref,
    par_ref,
    strength_ref,
    recip_ref,
    kfrac_ref,
    out_ref,
    occ_all,
    wave,
    stage,
    proj,
    occ_a,
    occ_b,
    coef,
    occ_coef,
    occ_tile,
    scaled,
    total,
    ys1,
    yr1,
    oyr,
    zs1,
    zr1,
    ys2,
    yr2,
    zs2,
    zr2,
    tile_send,
    tile_recv,
    tile_own,
    tiles,
    g_send,
    g_recv,
    y1_send,
    y1_recv,
    oy_send,
    oy_recv,
    ts_send,
    ts_recv,
    z1_send,
    z1_recv,
    y2_send,
    y2_recv,
    z2_send,
    z2_recv,
    t_send,
    t_recv,
):
    p = lax.axis_index("pw")
    b = lax.axis_index("band")
    nband = 4 * nx
    y_lo, z = p // nz, p % nz
    y_hi, x, core = b // (2 * nx), (b // 2) % nx, b % 2
    width = high_ref.shape[2]

    def band_id(yy, xx, cc):
        return yy * (2 * nx) + xx * 2 + cc

    def pw_id(yy, zz):
        return yy * nz + zz

    def put(src, dst, send, recv, pw, band):
        return pltpu.make_async_remote_copy(
            src_ref=src,
            dst_ref=dst,
            send_sem=send,
            recv_sem=recv,
            device_id={"pw": pw, "band": band},
            device_id_type=MESH,
        )

    y_mate = pw_id(1 - y_lo, z)

    def z_at(offset):
        return pw_id(y_lo, (z + offset + nz) % nz)


    barrier = pltpu.get_barrier_semaphore()
    pl.semaphore_signal(barrier, inc=1, device_id={"pw": y_mate, "band": b}, device_id_type=MESH)
    for step in range(1, nz):
        pl.semaphore_signal(
            barrier, inc=1, device_id={"pw": z_at(step), "band": b}, device_id_type=MESH
        )
    for step in range(1, nband):
        pl.semaphore_signal(
            barrier, inc=1, device_id={"pw": p, "band": (b + step) % nband}, device_id_type=MESH
        )

    shifted = [miller_ref[axis : axis + 1, :].astype(F32) + kfrac_ref[axis] for axis in range(3)]
    vectors = [
        shifted[0] * recip_ref[0, axis] + shifted[1] * recip_ref[1, axis] + shifted[2] * recip_ref[2, axis]
        for axis in range(3)
    ]
    for axis in range(3):
        wave[axis] = jnp.broadcast_to(vectors[axis], (8, width))
    wave[3] = jnp.broadcast_to(
        vectors[0] * vectors[0] + vectors[1] * vectors[1] + vectors[2] * vectors[2], (8, width)
    )
    nown = occ_ref.shape[1]
    occ_a[...] = jnp.zeros_like(occ_a)
    occ_b[...] = jnp.zeros_like(occ_b)
    occ_a[0:nown, :] = occ_ref[0]
    occ_a[nown : 2 * nown, :] = occ_ref[1]
    occ_b[0:nown, :] = occ_ref[1]
    occ_b[nown : 2 * nown, :] = -occ_ref[0]

    channel = lax.broadcasted_iota(jnp.int32, (8, LANES), 0) % 4
    selectors = [(channel == value).astype(F32) for value in range(4)]
    pieces = width // LANES

    def place(part, kind, value):
        for piece in range(LANES // 128):
            stage[part, piece, pl.ds(kind, 8, stride=4), :] = value[:, 128 * piece : 128 * piece + 128]

    def build(index, carry):
        block = index // pieces
        columns = pl.ds(pl.multiple_of((index % pieces) * LANES, LANES), LANES)
        table = par_ref[pl.ds(pl.multiple_of(block * 8, 8), 8), :]
        k = [wave[axis, :, columns] for axis in range(3)]
        square = wave[3, :, columns]
        spread = table[:, 3:4]
        envelope = jnp.exp(-0.5 * spread * square)
        angular = selectors[0] + selectors[1] * k[0] + selectors[2] * k[1] + selectors[3] * k[2]
        sine, cosine = sin_cos(table[:, 0:1] * k[0] + table[:, 1:2] * k[1] + table[:, 2:3] * k[2])
        radial = envelope * angular
        place(0, 0, radial * cosine)
        place(1, 0, -radial * sine)
        for axis in range(3):
            factor = envelope * (selectors[axis + 1] - spread * k[axis] * angular)
            place(0, axis + 1, factor * sine)
            place(1, axis + 1, factor * cosine)
        rows = pl.ds(pl.multiple_of(block * 32, 32), 32)
        for part in range(2):
            pieces_of = [stage[part, piece] for piece in range(LANES // 128)]
            proj[part, rows, columns] = jnp.concatenate(pieces_of, axis=1).astype(BF16)
        return carry

    lax.fori_loop(0, (par_ref.shape[0] // 8) * pieces, build, 0)

    pl.semaphore_wait(barrier, nz + nband - 1)

    started = []

    def forward(src, block, count, bands):
        for band in bands:
            copy = put(src, occ_all.at[block], g_send.at[count], g_recv.at[block], p, band)
            copy.start()
            started.append(copy)
            count += 1
        return count

    def block_arrived(block):
        put(occ_all.at[block], occ_all.at[block], g_send.at[0], g_recv.at[block], p, b).wait_recv()

    mate_block = band_id(1 - y_hi, x, core)
    x_others = [(x + dx) % nx for dx in range(1, nx)]
    sent = forward(
        occ_ref,
        b,
        0,
        [mate_block] + [band_id(y_hi, xx, core) for xx in x_others] + [band_id(y_hi, x, 1 - core)],
    )
    occ_all[b] = occ_ref[...]

    coef[...] = jnp.zeros_like(coef)
    occ_coef[...] = jnp.zeros_like(occ_coef)

    def project_occ(index, carry):
        columns = pl.ds(pl.multiple_of(index * 256, 256), 256)
        occ_coef[...] += dot_t(proj[0, :, columns], occ_a[:, columns]) + dot_t(
            proj[1, :, columns], occ_b[:, columns]
        )
        return carry

    lax.fori_loop(0, width // 256, project_occ, 0)
    npw = 2 * nz
    for owner in range(npw):
        rows = occ_coef[24 * owner : 24 * owner + 24, :] * strength_ref[24 * owner : 24 * owner + 24, :]
        occ_tile[owner] = (
            rows[0:8] + pltpu.roll(rows[8:16], 32, 1) + pltpu.roll(rows[16:24], 64, 1)
        )
    tile_copy = put(
        occ_tile.at[pl.ds((1 - y_lo) * nz, nz)], oyr, oy_send.at[0], oy_recv.at[0], y_mate, b
    )
    tile_copy.start()
    block_arrived(mate_block)
    sent = forward(
        occ_all.at[mate_block],
        mate_block,
        sent,
        [band_id(y_hi, xx, core) for xx in x_others] + [band_id(y_hi, x, 1 - core)],
    )

    def project(index, carry):
        columns = pl.ds(pl.multiple_of(index * 256, 256), 256)
        real, imag = proj[0, :, columns], proj[1, :, columns]
        high_r, high_i = high_ref[0, :, columns], high_ref[1, :, columns]
        coef[0] += dot_t(real, high_r) + dot_t(imag, high_i)
        coef[1] += dot_t(real, high_i) - dot_t(imag, high_r)
        return carry

    lax.fori_loop(0, width // 256, project, 0)

    def chunk1(owner):
        return coef[:, pl.ds(pl.multiple_of(owner * 24, 8), 24), :].reshape(48, 256)

    def chunk2(owner):
        return total[:, :, pl.ds(pl.multiple_of(owner * 8, 8), 8), :].reshape(48, 256)

    def mate_sends(chunk, ys, yr, send, recv):
        copies = []
        for place, offset in enumerate(ORDER):
            ys[place] = chunk(pw_id(1 - y_lo, (z + offset + nz) % nz)).astype(BF16)
            copy = put(ys.at[place], yr.at[place], send.at[place], recv.at[place], y_mate, b)
            copy.start()
            copies.append(copy)
        return copies

    def reduce_z(chunk, mates, yr, zs, zr, send, recv, fill):
        copies = {}

        def local(offset):
            place = ORDER.index(offset)
            mates[place].wait_recv()
            return chunk(z_at(offset)) + yr[place].astype(F32)

        def push(slot, value, offset):
            zs[slot] = value.astype(BF16)
            copy = put(zs.at[slot], zr.at[slot], send.at[slot], recv.at[slot], z_at(offset), b)
            copy.start()
            copies[slot] = copy

        def arrived(slot):
            copies[slot].wait_recv()
            return zr[slot].astype(F32)

        for slot, (offset, target) in enumerate(MOVES):
            push(slot, local(offset), target)
        relayed = [local(offset) for offset in RELAYS]
        for place, offset in enumerate(DIRECT):
            push(len(MOVES) + place, local(offset), offset)
        fill(0)
        for place, offset in enumerate(RELAYS):
            value = relayed[place]
            for slot, (_, target) in enumerate(MOVES):
                if target * offset > 0:
                    value = value + arrived(slot)
            push(len(MOVES) + len(DIRECT) + place, value, offset)
        fill(1)
        value = local(0)
        for place in range(len(DIRECT) + len(RELAYS)):
            value = value + arrived(len(MOVES) + place)
        return value, list(copies.values())

    mates1 = mate_sends(chunk1, ys1, yr1, y1_send, y1_recv)
    tile_copy.wait_recv()
    spread_copies = []
    for step in range(1, nz):
        dest = (z + step) % nz
        tile_send[step] = occ_tile[pw_id(y_lo, dest)] + oyr[dest]
        copy = put(
            tile_send.at[step], tile_recv.at[step], ts_send.at[step], ts_recv.at[step], z_at(step), b
        )
        copy.start()
        spread_copies.append(copy)
    for yy in (y_hi, 1 - y_hi):
        for xx in x_others:
            block = band_id(yy, xx, core)
            block_arrived(block)
            sent = forward(occ_all.at[block], block, sent, [band_id(y_hi, x, 1 - core)])
    total[...] = jnp.zeros_like(total)

    nocc = total.shape[2]

    def momentum_piece(index):
        columns = pl.ds(pl.multiple_of(index * 256, 256), 256)
        for part in range(2):
            values = occ_all[:, part, :, columns].reshape(nocc, 256).astype(F32)
            for axis in range(3):
                vector = wave[axis, 0:1, columns]
                scaled[part, axis * nocc : (axis + 1) * nocc, :] = (values * vector).astype(BF16)
        real, imag = scaled[0], scaled[1]
        high_r, high_i = high_ref[0, :, columns], high_ref[1, :, columns]
        total[0] += (dot_t(real, high_r) + dot_t(imag, high_i)).reshape(3, nocc, 256)
        total[1] += (dot_t(real, high_i) - dot_t(imag, high_r)).reshape(3, nocc, 256)

    tile_copies = []

    def fill1(point):
        if point == 0:
            tile = occ_tile[p] + oyr[z]
            for copy, step in zip(spread_copies, range(1, nz)):
                copy.wait_recv()
                tile = tile + tile_recv[step]
            tile_own[...] = tile
            for step in range(1, nband):
                copy = put(
                    tile_own, tiles.at[b], t_send.at[step - 1], t_recv.at[b], p, (b + step) % nband
                )
                copy.start()
                tile_copies.append(copy)
            tiles[b] = tile
            for xx in [x] + x_others:
                for yy in range(2):
                    block_arrived(band_id(yy, xx, 1 - core))
            momentum_piece(0)
            momentum_piece(1)
        else:
            for index in range(2, width // 256):
                momentum_piece(index)

    high_sum, moves1 = reduce_z(chunk1, mates1, yr1, zs1, zr1, z1_send, z1_recv, fill1)

    high_hi = high_sum.astype(BF16)
    high_lo = (high_sum - high_hi.astype(F32)).astype(BF16)
    rhs = jnp.concatenate([high_hi, high_lo, high_hi], axis=0)
    for step in range(1, nband):
        block = (b + step) % nband
        put(tile_own, tiles.at[block], t_send.at[0], t_recv.at[block], p, b).wait_recv()

    lane_block = lax.broadcasted_iota(jnp.int32, (8, 128), 1) // 16
    occ_sums = []
    for part in range(2):
        groups = []
        for group in range(3):
            halves = []
            for side in range(nband // 8):
                value = jnp.zeros((8, 128), F32)
                for place in range(8):
                    shift = (16 * place - 32 * group - 16 * part) % 128
                    tile = tiles[8 * side + place]
                    if shift:
                        tile = pltpu.roll(tile, shift, 1)
                    value = jnp.where(lane_block == place, tile, value)
                halves.append(value)
            groups.append(jnp.concatenate(halves, axis=1))
        occ_sums.append(jnp.concatenate(groups, axis=0))
    kind = lax.broadcasted_iota(jnp.int32, (24, 256), 0) % 4
    for axis in range(3):
        mixed = []
        for part in range(2):
            value = occ_sums[part]
            lower = pltpu.roll(value, axis + 1, 0)
            upper = pltpu.roll(value, 24 - (axis + 1), 0)
            mixed.append(
                jnp.where(kind == axis + 1, lower, jnp.where(kind == 0, -upper, jnp.zeros_like(value)))
            )
        for part in range(2):
            if part == 0:
                left = jnp.concatenate([mixed[1], -mixed[0]], axis=0)
            else:
                left = jnp.concatenate([mixed[0], mixed[1]], axis=0)
            left_hi = left.astype(BF16)
            left_lo = (left - left_hi.astype(F32)).astype(BF16)
            lhs = jnp.concatenate([left_hi, left_hi, left_lo], axis=0)
            total[part, axis] += lax.dot_general(
                lhs, rhs, (((0,), (0,)), ((), ())), preferred_element_type=F32
            )

    mates2 = mate_sends(chunk2, ys2, yr2, y2_send, y2_recv)
    result, moves2 = reduce_z(
        chunk2, mates2, yr2, zs2, zr2, z2_send, z2_recv, lambda point: None
    )
    result = result.reshape(2, 3, 8, 256)
    for axis in range(3):
        for part in range(2):
            out_ref[axis, part] = result[part, axis]

    for copy in (
        started + [tile_copy] + mates1 + spread_copies + moves1 + tile_copies + mates2 + moves2
    ):
        copy.wait_send()


def on_device(
    nz, nx, psi_occ, psi_high, miller, recip, kfrac, positions, atom_type, proj_atom, widths, dion
):
    nproj = proj_atom.shape[0]
    nown, nhigh, width = psi_occ.shape[1], psi_high.shape[1], psi_high.shape[2]
    npw, nband = 2 * nz, 4 * nx
    nocc = nown * nband
    table = projector_table(positions, atom_type, proj_atom, widths, dion)
    strength = jnp.broadcast_to(jnp.repeat(table[:, 4:5], 4, axis=0), (4 * nproj, 128))
    vmem, smem = pltpu.VMEM, pltpu.SMEM
    dma = pltpu.SemaphoreType.DMA
    out = pl.pallas_call(
        functools.partial(kernel, nz, nx),
        out_shape=jax.ShapeDtypeStruct((3, 2, nocc // npw, nhigh), F32),
        in_specs=[pl.BlockSpec(memory_space=vmem)] * 5 + [pl.BlockSpec(memory_space=smem)] * 2,
        out_specs=pl.BlockSpec(memory_space=vmem),
        scratch_shapes=[
            vmem((nband, 2, nown, width), BF16),
            vmem((4, 8, width), F32),
            vmem((2, LANES // 128, 32, 128), F32),
            vmem((2, 4 * nproj, width), BF16),
            vmem((128, width), BF16),
            vmem((128, width), BF16),
            vmem((2, 4 * nproj, nhigh), F32),
            vmem((4 * nproj, 128), F32),
            vmem((npw, 8, 128), F32),
            vmem((2, 3 * nocc, 256), BF16),
            vmem((2, 3, nocc, nhigh), F32),
            vmem((nz, 48, nhigh), BF16),
            vmem((nz, 48, nhigh), BF16),
            vmem((nz, 8, 128), F32),
            vmem((nz - 1, 48, nhigh), BF16),
            vmem((nz - 1, 48, nhigh), BF16),
            vmem((nz, 48, nhigh), BF16),
            vmem((nz, 48, nhigh), BF16),
            vmem((nz - 1, 48, nhigh), BF16),
            vmem((nz - 1, 48, nhigh), BF16),
            vmem((nz, 8, 128), F32),
            vmem((nz, 8, 128), F32),
            vmem((8, 128), F32),
            vmem((nband, 8, 128), F32),
            dma((nband - 1,)),
            dma((nband,)),
            dma((nz,)),
            dma((nz,)),
            dma((1,)),
            dma((1,)),
            dma((nz,)),
            dma((nz,)),
            dma((nz - 1,)),
            dma((nz - 1,)),
            dma((nz,)),
            dma((nz,)),
            dma((nz - 1,)),
            dma((nz - 1,)),
            dma((nband - 1,)),
            dma((nband,)),
        ],
        compiler_params=pltpu.CompilerParams(
            collective_id=0, has_side_effects=True, vmem_limit_bytes=52 * 1024 * 1024
        ),
    )(psi_occ, psi_high, miller, table, strength, recip, kfrac)
    return out


def solution(mesh):
    nz = mesh.shape["pw"] // 2
    nx = mesh.shape["band"] // 4
    placed = (
        P(None, "band", "pw"),
        P(None, "band", "pw"),
        P(None, "pw"),
        P(),
        P(),
        P(),
        P(),
        P(),
        P(),
        P(),
    )
    return jax.shard_map(
        functools.partial(on_device, nz, nx),
        mesh=mesh,
        in_specs=placed,
        out_specs=P(None, None, "pw", "band"),
        check_vma=False,
    )
```

```python
import functools

import jax
import jax.numpy as jnp
from jax import lax
from jax.experimental import pallas as pl
from jax.experimental.pallas import tpu as pltpu
from jax.sharding import PartitionSpec as P

MESH = pl.DeviceIdType.MESH
F32 = jnp.float32
BF16 = jnp.bfloat16
LANES = 512
MOVES = [(8, 4), (-7, -3), (7, 3), (-6, -2), (6, 2), (-5, -1), (5, 1)]
RELAYS = [4, -4]
DIRECT = [3, -3, 2, -2, 1, -1]
ORDER = [offset for offset, _ in MOVES] + RELAYS + DIRECT + [0]


def sin_cos(angle):
    turns = jnp.floor(angle * 0.6366197723675814 + 0.5)
    rest = angle - turns * 1.5703125
    rest = rest - turns * 4.837512969970703125e-4
    rest = rest - turns * 7.54978995489188216e-8
    square = rest * rest
    sine = rest + rest * square * (
        -1.6666654611e-1 + square * (8.3321608736e-3 + square * -1.9515295891e-4)
    )
    cosine = (
        1.0
        - 0.5 * square
        + square * square * (4.166664568298827e-2 + square * (-1.388731625493765e-3 + square * 2.443315711809948e-5))
    )
    quadrant = turns - 4.0 * jnp.floor(turns * 0.25)
    odd = (quadrant == 1.0) | (quadrant == 3.0)
    first = jnp.where(odd, cosine, sine)
    second = jnp.where(odd, sine, cosine)
    sine = jnp.where(quadrant >= 2.0, -first, first)
    cosine = jnp.where((quadrant == 1.0) | (quadrant == 2.0), -second, second)
    return sine, cosine


def dot_t(lhs, rhs):
    return lax.dot_general(lhs, rhs, (((1,), (1,)), ((), ())), preferred_element_type=F32)


def kernel(
    nz,
    nx,
    occ_hbm,
    high_hbm,
    miller_hbm,
    recip_hbm,
    kfrac_hbm,
    positions_hbm,
    atom_type_hbm,
    proj_atom_hbm,
    widths_hbm,
    dion_hbm,
    out_ref,
    high_ref,
    miller_ref,
    recip_ref,
    kfrac_ref,
    positions_ref,
    atom_type_ref,
    proj_atom_ref,
    widths_ref,
    dion_ref,
    in_sem,
    occ_all,
    wave,
    waves,
    radial,
    pick_cos,
    pick_sin,
    type_hot,
    strength_ref,
    proj,
    lefts,
    occ_a,
    occ_b,
    coef,
    occ_coef,
    occ_tile,
    scaled,
    total,
    ys1,
    yr1,
    oyr,
    zs1,
    zr1,
    ys2,
    yr2,
    zs2,
    zr2,
    tile_send,
    tile_recv,
    tile_own,
    tiles,
    g_send,
    g_recv,
    y1_send,
    y1_recv,
    oy_send,
    oy_recv,
    ts_send,
    ts_recv,
    z1_send,
    z1_recv,
    y2_send,
    y2_recv,
    z2_send,
    z2_recv,
    t_send,
    t_recv,
):
    p = lax.axis_index("pw")
    b = lax.axis_index("band")
    nband = 4 * nx
    y_lo, z = p // nz, p % nz
    y_hi, x, core = b // (2 * nx), (b // 2) % nx, b % 2
    width, nown = high_hbm.shape[2], occ_hbm.shape[1]

    def band_id(yy, xx, cc):
        return yy * (2 * nx) + xx * 2 + cc

    def pw_id(yy, zz):
        return yy * nz + zz

    def put(src, dst, send, recv, pw, band):
        return pltpu.make_async_remote_copy(
            src_ref=src,
            dst_ref=dst,
            send_sem=send,
            recv_sem=recv,
            device_id={"pw": pw, "band": band},
            device_id_type=MESH,
        )

    y_mate = pw_id(1 - y_lo, z)

    def z_at(offset):
        return pw_id(y_lo, (z + offset + nz) % nz)


    sources = (
        (occ_hbm, occ_all.at[b]),
        (high_hbm, high_ref),
        (miller_hbm, miller_ref),
        (recip_hbm, recip_ref),
        (kfrac_hbm, kfrac_ref),
        (positions_hbm, positions_ref),
        (atom_type_hbm, atom_type_ref),
        (proj_atom_hbm, proj_atom_ref),
        (widths_hbm, widths_ref),
        (dion_hbm, dion_ref),
    )
    loads = [
        pltpu.make_async_copy(src, dst, in_sem.at[place]) for place, (src, dst) in enumerate(sources)
    ]
    for copy in loads[2:] + loads[:2]:
        copy.start()
    barrier = pltpu.get_barrier_semaphore()
    pl.semaphore_signal(barrier, inc=1, device_id={"pw": y_mate, "band": b}, device_id_type=MESH)
    for step in range(1, nz):
        pl.semaphore_signal(
            barrier, inc=1, device_id={"pw": z_at(step), "band": b}, device_id_type=MESH
        )
    for step in range(1, nband):
        pl.semaphore_signal(
            barrier, inc=1, device_id={"pw": p, "band": (b + step) % nband}, device_id_type=MESH
        )

    for copy in loads[2:]:
        copy.wait()
    shifted = [
        miller_ref[axis : axis + 1, :].astype(F32) + kfrac_ref[0:1, axis : axis + 1] for axis in range(3)
    ]
    vectors = [
        shifted[0] * recip_ref[0:1, axis : axis + 1]
        + shifted[1] * recip_ref[1:2, axis : axis + 1]
        + shifted[2] * recip_ref[2:3, axis : axis + 1]
        for axis in range(3)
    ]
    for axis in range(3):
        wave[axis] = jnp.broadcast_to(vectors[axis], (8, width))
    wave[3] = jnp.broadcast_to(
        vectors[0] * vectors[0] + vectors[1] * vectors[1] + vectors[2] * vectors[2], (8, width)
    )

    nproj, natom, ntype = proj_atom_ref.shape[1], atom_type_ref.shape[1], widths_ref.shape[1]
    nrow = 4 * nproj
    atoms = lax.rem(lax.broadcasted_iota(jnp.int32, (4 * natom, nproj), 0), natom)
    atom_hot = (atoms == proj_atom_ref[...]).astype(F32).astype(BF16)
    row_of = lax.broadcasted_iota(jnp.int32, (nrow, nproj), 0) // 4
    row_hot = (row_of == lax.broadcasted_iota(jnp.int32, (nrow, nproj), 1)).astype(F32).astype(BF16)
    hot = dot_t(row_hot, atom_hot)
    types = lax.broadcasted_iota(jnp.int32, (8, natom), 0)
    of_type = (types == atom_type_ref[...]).astype(F32)
    by_type = dot_t(hot[:, 0:natom].astype(BF16), of_type.astype(BF16))
    type_hot[...] = by_type
    weight = by_type[:, 0:1] * dion_ref[0:1, 0:1]
    for value in range(1, ntype):
        weight = weight + by_type[:, value : value + 1] * dion_ref[0:1, value : value + 1]
    strength_ref[...] = jnp.broadcast_to(weight, (nrow, 128))
    is_value = lax.rem(lax.broadcasted_iota(jnp.int32, (nrow, 4 * natom), 0), 4) == 0
    in_cos = lax.broadcasted_iota(jnp.int32, (nrow, 4 * natom), 1) < 2 * natom
    zero = jnp.zeros_like(hot)
    pick_cos[...] = jnp.where(is_value == in_cos, hot, zero).astype(BF16)
    pick_sin[...] = jnp.where(is_value, jnp.where(in_cos, zero, -hot), jnp.where(in_cos, hot, zero)).astype(
        BF16
    )

    centers = positions_ref[...].T
    row = lax.broadcasted_iota(jnp.int32, (8, LANES), 0)

    def tables(index, carry):
        columns = pl.ds(pl.multiple_of(index * LANES, LANES), LANES)
        k = [wave[axis, :, columns] for axis in range(4)]
        for first in range(0, natom, 16):
            parts = []
            for begin in (first, first + 8):
                place = centers[begin : begin + 8]
                parts.append(sin_cos(place[:, 0:1] * k[0] + place[:, 1:2] * k[1] + place[:, 2:3] * k[2]))
            for block, which in ((0, 1), (2, 0)):
                value = jnp.concatenate([parts[0][which], parts[1][which]], axis=0)
                upper = value.astype(BF16)
                waves[block * natom + first : block * natom + first + 16, columns] = upper
                waves[(block + 1) * natom + first : (block + 1) * natom + first + 16, columns] = (
                    value - upper.astype(F32)
                ).astype(BF16)
        kind = lax.rem(row, 4)
        along = jnp.where(kind == 1, k[0], jnp.where(kind == 2, k[1], k[2]))
        for value in range(ntype):
            spread = widths_ref[0:1, value : value + 1]
            envelope = jnp.exp(-0.5 * spread * k[3])
            for pair in range(2):
                channel = 2 * pair + row // 4
                if pair == 0:
                    angular = jnp.where(channel == 0, jnp.ones_like(along), k[0])
                else:
                    angular = jnp.where(channel == 2, k[1], k[2])
                matching = ((channel == kind) & (kind > 0)).astype(F32)
                factor = jnp.where(kind == 0, angular, matching - spread * along * angular)
                radial[value, 8 * pair : 8 * pair + 8, columns] = envelope * factor
        return carry

    lax.fori_loop(0, width // LANES, tables, 0)

    hrow = nrow // 2

    def build(half):
        rows = pl.ds(pl.multiple_of(half * hrow, hrow), hrow)
        left_cos, left_sin = pick_cos[rows, :], pick_sin[rows, :]
        kinds = type_hot[rows, :]

        def tile(index, carry):
            columns = pl.ds(pl.multiple_of(index * 256, 256), 256)
            right = waves[:, columns]
            table = [
                jnp.broadcast_to(radial[value, :, columns][None], (hrow // 16, 16, 256)).reshape(hrow, 256)
                for value in range(ntype)
            ]
            part = table[0]
            for value in range(1, ntype):
                part = jnp.where(kinds[:, value : value + 1] > 0.5, table[value], part)
            proj[0, rows, columns] = (part * jnp.dot(left_cos, right, preferred_element_type=F32)).astype(BF16)
            proj[1, rows, columns] = (part * jnp.dot(left_sin, right, preferred_element_type=F32)).astype(BF16)
            return carry

        lax.fori_loop(0, width // 256, tile, 0)

    build(1 - y_lo)
    for copy in loads[:2]:
        copy.wait()
    pl.semaphore_wait(barrier, nz + nband - 1)

    started = []

    def forward(src, block, count, bands):
        for band in bands:
            copy = put(src, occ_all.at[block], g_send.at[count], g_recv.at[block], p, band)
            copy.start()
            started.append(copy)
            count += 1
        return count

    def block_arrived(block):
        put(occ_all.at[block], occ_all.at[block], g_send.at[0], g_recv.at[block], p, b).wait_recv()

    mate_block = band_id(1 - y_hi, x, core)
    x_others = [(x + dx) % nx for dx in range(1, nx)]
    sent = forward(
        occ_all.at[b],
        b,
        0,
        [mate_block] + [band_id(y_hi, xx, core) for xx in x_others] + [band_id(y_hi, x, 1 - core)],
    )

    def project(half):
        rows = pl.ds(pl.multiple_of(half * hrow, hrow), hrow)
        real, imag = proj[0, rows, :], proj[1, rows, :]
        coef[0, rows, :] = dot_t(real, high_ref[0]) + dot_t(imag, high_ref[1])
        coef[1, rows, :] = dot_t(real, high_ref[1]) - dot_t(imag, high_ref[0])

    project(1 - y_lo)

    def chunk1(owner):
        return coef[:, pl.ds(pl.multiple_of(owner * 24, 8), 24), :].reshape(48, 256)

    def chunk2(owner):
        return total[:, :, pl.ds(pl.multiple_of(owner * 8, 8), 8), :].reshape(48, 256)

    def mate_sends(chunk, ys, yr, send, recv):
        copies = []
        for place, offset in enumerate(ORDER):
            ys[place] = chunk(pw_id(1 - y_lo, (z + offset + nz) % nz)).astype(BF16)
            copy = put(ys.at[place], yr.at[place], send.at[place], recv.at[place], y_mate, b)
            copy.start()
            copies.append(copy)
        return copies

    def reduce_z(chunk, mates, yr, zs, zr, send, recv, fill):
        copies = {}

        def local(offset):
            place = ORDER.index(offset)
            mates[place].wait_recv()
            return chunk(z_at(offset)) + yr[place].astype(F32)

        def push(slot, value, offset):
            zs[slot] = value.astype(BF16)
            copy = put(zs.at[slot], zr.at[slot], send.at[slot], recv.at[slot], z_at(offset), b)
            copy.start()
            copies[slot] = copy

        def arrived(slot):
            copies[slot].wait_recv()
            return zr[slot].astype(F32)

        for slot, (offset, target) in enumerate(MOVES):
            push(slot, local(offset), target)
        fill(0)
        relayed = [local(offset) for offset in RELAYS]
        for place, offset in enumerate(DIRECT):
            push(len(MOVES) + place, local(offset), offset)
        fill(1)
        for place, offset in enumerate(RELAYS):
            value = relayed[place]
            for slot, (_, target) in enumerate(MOVES):
                if target * offset > 0:
                    value = value + arrived(slot)
            push(len(MOVES) + len(DIRECT) + place, value, offset)
        fill(2)
        value = local(0)
        for place in range(len(DIRECT) + len(RELAYS)):
            value = value + arrived(len(MOVES) + place)
        return value, list(copies.values())

    mates1 = mate_sends(chunk1, ys1, yr1, y1_send, y1_recv)
    build(y_lo)
    project(y_lo)
    block_arrived(mate_block)
    sent = forward(
        occ_all.at[mate_block],
        mate_block,
        sent,
        [band_id(y_hi, xx, core) for xx in x_others] + [band_id(y_hi, x, 1 - core)],
    )
    occ_a[...] = jnp.zeros_like(occ_a)
    occ_b[...] = jnp.zeros_like(occ_b)
    occ_a[0:nown, :] = occ_all[b, 0]
    occ_a[nown : 2 * nown, :] = occ_all[b, 1]
    occ_b[0:nown, :] = occ_all[b, 1]
    occ_b[nown : 2 * nown, :] = -occ_all[b, 0]
    occ_coef[...] = dot_t(proj[0], occ_a[...]) + dot_t(proj[1], occ_b[...])
    for owner in range(2 * nz):
        rows = occ_coef[24 * owner : 24 * owner + 24, :] * strength_ref[24 * owner : 24 * owner + 24, :]
        occ_tile[owner] = (
            rows[0:8] + pltpu.roll(rows[8:16], 32, 1) + pltpu.roll(rows[16:24], 64, 1)
        )
    tile_copy = put(
        occ_tile.at[pl.ds((1 - y_lo) * nz, nz)], oyr, oy_send.at[0], oy_recv.at[0], y_mate, b
    )
    tile_copy.start()

    nocc = total.shape[2]

    def momentum_piece(index):
        columns = pl.ds(pl.multiple_of(index * 256, 256), 256)
        for part in range(2):
            values = occ_all[:, part, :, columns].reshape(nocc, 256).astype(F32)
            for axis in range(3):
                vector = wave[axis, 0:1, columns]
                scaled[part, axis * nocc : (axis + 1) * nocc, :] = (values * vector).astype(BF16)
        real, imag = scaled[0], scaled[1]
        high_r, high_i = high_ref[0, :, columns], high_ref[1, :, columns]
        parts = (
            dot_t(real, high_r) + dot_t(imag, high_i),
            dot_t(real, high_i) - dot_t(imag, high_r),
        )
        for part in range(2):
            value = parts[part].reshape(3, nocc, 256)
            if index == 0:
                total[part] = value
            else:
                total[part] += value

    tile_copies = []
    spread_copies = []

    def fill1(point):
        nonlocal sent
        if point == 0:
            tile_copy.wait_recv()
            for step in range(1, nz):
                dest = (z + step) % nz
                tile_send[step] = occ_tile[pw_id(y_lo, dest)] + oyr[dest]
                copy = put(
                    tile_send.at[step],
                    tile_recv.at[step],
                    ts_send.at[step],
                    ts_recv.at[step],
                    z_at(step),
                    b,
                )
                copy.start()
                spread_copies.append(copy)
            for yy in (y_hi, 1 - y_hi):
                for xx in x_others:
                    block = band_id(yy, xx, core)
                    block_arrived(block)
                    sent = forward(occ_all.at[block], block, sent, [band_id(y_hi, x, 1 - core)])
        elif point == 1:
            for xx in [x] + x_others:
                for yy in range(2):
                    block_arrived(band_id(yy, xx, 1 - core))
            for index in range(3):
                momentum_piece(index)
        else:
            tile = occ_tile[p] + oyr[z]
            for copy, step in zip(spread_copies, range(1, nz)):
                copy.wait_recv()
                tile = tile + tile_recv[step]
            tile_own[...] = tile
            for step in range(1, nband):
                copy = put(
                    tile_own, tiles.at[b], t_send.at[step - 1], t_recv.at[b], p, (b + step) % nband
                )
                copy.start()
                tile_copies.append(copy)
            tiles[b] = tile
            for index in range(3, width // 256):
                momentum_piece(index)

    high_sum, moves1 = reduce_z(chunk1, mates1, yr1, zs1, zr1, z1_send, z1_recv, fill1)

    high_hi = high_sum.astype(BF16)
    high_lo = (high_sum - high_hi.astype(F32)).astype(BF16)
    rhs = jnp.concatenate([high_hi, high_lo, high_hi], axis=0)
    for step in range(1, nband):
        block = (b + step) % nband
        put(tile_own, tiles.at[block], t_send.at[0], t_recv.at[block], p, b).wait_recv()

    lane_block = lax.broadcasted_iota(jnp.int32, (8, 128), 1) // 16
    occ_sums = []
    for part in range(2):
        groups = []
        for group in range(3):
            halves = []
            for side in range(nband // 8):
                value = jnp.zeros((8, 128), F32)
                for place in range(8):
                    shift = (16 * place - 32 * group - 16 * part) % 128
                    tile = tiles[8 * side + place]
                    if shift:
                        tile = pltpu.roll(tile, shift, 1)
                    value = jnp.where(lane_block == place, tile, value)
                halves.append(value)
            groups.append(jnp.concatenate(halves, axis=1))
        occ_sums.append(jnp.concatenate(groups, axis=0))
    kind = lax.broadcasted_iota(jnp.int32, (24, 256), 0) % 4
    for axis in range(3):
        mixed = []
        for part in range(2):
            value = occ_sums[part]
            lower = pltpu.roll(value, axis + 1, 0)
            upper = pltpu.roll(value, 24 - (axis + 1), 0)
            mixed.append(
                jnp.where(kind == axis + 1, lower, jnp.where(kind == 0, -upper, jnp.zeros_like(value)))
            )
        for part in range(2):
            if part == 0:
                left = jnp.concatenate([mixed[1], -mixed[0]], axis=0)
            else:
                left = jnp.concatenate([mixed[0], mixed[1]], axis=0)
            left_hi = left.astype(BF16)
            left_lo = (left - left_hi.astype(F32)).astype(BF16)
            lhs = jnp.concatenate([left_hi, left_hi, left_lo], axis=0)
            lefts[3 * part + axis] = lhs

    def nonlocal_part(half):
        rows = pl.ds(pl.multiple_of(half * (nocc // 2), 128), nocc // 2)
        for part in range(2):
            for axis in range(3):
                total[part, axis, rows, :] += lax.dot_general(
                    lefts[3 * part + axis, :, rows], rhs, (((0,), (0,)), ((), ())), preferred_element_type=F32
                )

    nonlocal_part(1 - y_lo)
    mates2 = mate_sends(chunk2, ys2, yr2, y2_send, y2_recv)
    nonlocal_part(y_lo)
    result, moves2 = reduce_z(
        chunk2, mates2, yr2, zs2, zr2, z2_send, z2_recv, lambda point: None
    )
    result = result.reshape(2, 3, 8, 256)
    for axis in range(3):
        for part in range(2):
            out_ref[axis, part] = result[part, axis]

    for copy in (
        started + [tile_copy] + mates1 + spread_copies + moves1 + tile_copies + mates2 + moves2
    ):
        copy.wait_send()


def on_device(
    nz, nx, psi_occ, psi_high, miller, recip, kfrac, positions, atom_type, proj_atom, widths, dion
):
    nproj, natom, ntype = proj_atom.shape[0], positions.shape[0], widths.shape[0]
    nown, nhigh, width = psi_occ.shape[1], psi_high.shape[1], psi_high.shape[2]
    npw, nband = 2 * nz, 4 * nx
    nocc = nown * nband
    vmem = pltpu.VMEM
    dma = pltpu.SemaphoreType.DMA
    out = pl.pallas_call(
        functools.partial(kernel, nz, nx),
        out_shape=jax.ShapeDtypeStruct((3, 2, nocc // npw, nhigh), F32),
        in_specs=[pl.BlockSpec(memory_space=pltpu.HBM)] * 10,
        out_specs=pl.BlockSpec(memory_space=vmem),
        scratch_shapes=[
            vmem((2, nhigh, width), BF16),
            vmem((3, width), jnp.int32),
            vmem((3, 3), F32),
            vmem((1, 3), F32),
            vmem((3, natom), F32),
            vmem((1, natom), jnp.int32),
            vmem((1, nproj), jnp.int32),
            vmem((1, ntype), F32),
            vmem((1, ntype), F32),
            dma((10,)),
            vmem((nband, 2, nown, width), BF16),
            vmem((4, 8, width), F32),
            vmem((4 * natom, width), BF16),
            vmem((ntype, 16, width), F32),
            vmem((4 * nproj, 4 * natom), BF16),
            vmem((4 * nproj, 4 * natom), BF16),
            vmem((4 * nproj, 8), F32),
            vmem((4 * nproj, 128), F32),
            vmem((2, 4 * nproj, width), BF16),
            vmem((6, 144, nocc), BF16),
            vmem((128, width), BF16),
            vmem((128, width), BF16),
            vmem((2, 4 * nproj, nhigh), F32),
            vmem((4 * nproj, 128), F32),
            vmem((npw, 8, 128), F32),
            vmem((2, 3 * nocc, 256), BF16),
            vmem((2, 3, nocc, nhigh), F32),
            vmem((nz, 48, nhigh), BF16),
            vmem((nz, 48, nhigh), BF16),
            vmem((nz, 8, 128), F32),
            vmem((nz - 1, 48, nhigh), BF16),
            vmem((nz - 1, 48, nhigh), BF16),
            vmem((nz, 48, nhigh), BF16),
            vmem((nz, 48, nhigh), BF16),
            vmem((nz - 1, 48, nhigh), BF16),
            vmem((nz - 1, 48, nhigh), BF16),
            vmem((nz, 8, 128), F32),
            vmem((nz, 8, 128), F32),
            vmem((8, 128), F32),
            vmem((nband, 8, 128), F32),
            dma((nband - 1,)),
            dma((nband,)),
            dma((nz,)),
            dma((nz,)),
            dma((1,)),
            dma((1,)),
            dma((nz,)),
            dma((nz,)),
            dma((nz - 1,)),
            dma((nz - 1,)),
            dma((nz,)),
            dma((nz,)),
            dma((nz - 1,)),
            dma((nz - 1,)),
            dma((nband - 1,)),
            dma((nband,)),
        ],
        compiler_params=pltpu.CompilerParams(
            collective_id=0, has_side_effects=True, vmem_limit_bytes=52 * 1024 * 1024
        ),
    )(
        psi_occ,
        psi_high,
        miller,
        recip,
        kfrac[None],
        positions.T,
        atom_type[None],
        proj_atom[None],
        widths[None],
        dion[None],
    )
    return out


def solution(mesh):
    nz = mesh.shape["pw"] // 2
    nx = mesh.shape["band"] // 4
    placed = (
        P(None, "band", "pw"),
        P(None, "band", "pw"),
        P(None, "pw"),
        P(),
        P(),
        P(),
        P(),
        P(),
        P(),
        P(),
    )
    return jax.shard_map(
        functools.partial(on_device, nz, nx),
        mesh=mesh,
        in_specs=placed,
        out_specs=P(None, None, "pw", "band"),
        check_vma=False,
    )
```

```python
import functools

import jax
import jax.numpy as jnp
from jax import lax
from jax.experimental import pallas as pl
from jax.experimental.pallas import tpu as pltpu
from jax.sharding import PartitionSpec as P

MESH = pl.DeviceIdType.MESH
F32 = jnp.float32
BF16 = jnp.bfloat16
LANES = 512
MOVES = [(8, 4), (-7, -3), (7, 3), (-6, -2), (6, 2), (-5, -1), (5, 1)]
RELAYS = [4, -4]
DIRECT = [3, -3, 2, -2, 1, -1]
ORDER = [offset for offset, _ in MOVES] + RELAYS + DIRECT + [0]


def sin_cos(angle):
    turns = jnp.floor(angle * 0.6366197723675814 + 0.5)
    rest = angle - turns * 1.5703125
    rest = rest - turns * 4.837512969970703125e-4
    rest = rest - turns * 7.54978995489188216e-8
    square = rest * rest
    sine = rest + rest * square * (
        -1.6666654611e-1 + square * (8.3321608736e-3 + square * -1.9515295891e-4)
    )
    cosine = (
        1.0
        - 0.5 * square
        + square * square * (4.166664568298827e-2 + square * (-1.388731625493765e-3 + square * 2.443315711809948e-5))
    )
    quadrant = turns - 4.0 * jnp.floor(turns * 0.25)
    odd = (quadrant == 1.0) | (quadrant == 3.0)
    first = jnp.where(odd, cosine, sine)
    second = jnp.where(odd, sine, cosine)
    sine = jnp.where(quadrant >= 2.0, -first, first)
    cosine = jnp.where((quadrant == 1.0) | (quadrant == 2.0), -second, second)
    return sine, cosine


def dot_t(lhs, rhs):
    return lax.dot_general(lhs, rhs, (((1,), (1,)), ((), ())), preferred_element_type=F32)


def kernel(
    nz,
    nx,
    occ_hbm,
    high_hbm,
    miller_hbm,
    recip_hbm,
    kfrac_hbm,
    positions_hbm,
    atom_type_hbm,
    proj_atom_hbm,
    widths_hbm,
    dion_hbm,
    out_ref,
    high_ref,
    miller_ref,
    recip_ref,
    kfrac_ref,
    positions_ref,
    atom_type_ref,
    proj_atom_ref,
    widths_ref,
    dion_ref,
    in_sem,
    occ_all,
    wave,
    waves,
    radial,
    pick_cos,
    pick_sin,
    type_hot,
    strength_ref,
    proj,
    lefts,
    occ_a,
    occ_b,
    coef,
    occ_coef,
    occ_tile,
    scaled,
    total,
    ys1,
    yr1,
    zs1,
    zr1,
    ys2,
    yr2,
    zs2,
    zr2,
    tile_send,
    tile_recv,
    tile_own,
    tiles,
    g_send,
    g_recv,
    y1_send,
    y1_recv,
    ts_send,
    ts_recv,
    z1_send,
    z1_recv,
    y2_send,
    y2_recv,
    z2_send,
    z2_recv,
    t_send,
    t_recv,
):
    p = lax.axis_index("pw")
    b = lax.axis_index("band")
    nband = 4 * nx
    y_lo, z = p // nz, p % nz
    y_hi, x, core = b // (2 * nx), (b // 2) % nx, b % 2
    width, nown = high_hbm.shape[2], occ_hbm.shape[1]

    odd = z % 2

    def band_id(yy, xx, cc):
        return yy * (2 * nx) + xx * 2 + cc

    def pw_id(yy, zz):
        return yy * nz + zz

    def put(src, dst, send, recv, pw, band):
        return pltpu.make_async_remote_copy(
            src_ref=src,
            dst_ref=dst,
            send_sem=send,
            recv_sem=recv,
            device_id={"pw": pw, "band": band},
            device_id_type=MESH,
        )

    y_mate = pw_id(1 - y_lo, z)

    def z_at(offset):
        return pw_id(y_lo, (z + offset + nz) % nz)


    sources = (
        (occ_hbm, occ_all.at[b]),
        (high_hbm, high_ref),
        (miller_hbm, miller_ref),
        (recip_hbm, recip_ref),
        (kfrac_hbm, kfrac_ref),
        (positions_hbm, positions_ref),
        (atom_type_hbm, atom_type_ref),
        (proj_atom_hbm, proj_atom_ref),
        (widths_hbm, widths_ref),
        (dion_hbm, dion_ref),
    )
    loads = [
        pltpu.make_async_copy(src, dst, in_sem.at[place]) for place, (src, dst) in enumerate(sources)
    ]
    for copy in loads[2:] + loads[:2]:
        copy.start()
    barrier = pltpu.get_barrier_semaphore()
    for step in range(nband):
        pl.semaphore_signal(
            barrier, inc=1, device_id={"pw": y_mate, "band": (b + step) % nband}, device_id_type=MESH
        )
    for step in range(1, nz):
        pl.semaphore_signal(
            barrier, inc=1, device_id={"pw": z_at(step), "band": b}, device_id_type=MESH
        )
    for step in range(1, nband):
        pl.semaphore_signal(
            barrier, inc=1, device_id={"pw": p, "band": (b + step) % nband}, device_id_type=MESH
        )

    for copy in loads[2:]:
        copy.wait()
    shifted = [
        miller_ref[axis : axis + 1, :].astype(F32) + kfrac_ref[0:1, axis : axis + 1] for axis in range(3)
    ]
    vectors = [
        shifted[0] * recip_ref[0:1, axis : axis + 1]
        + shifted[1] * recip_ref[1:2, axis : axis + 1]
        + shifted[2] * recip_ref[2:3, axis : axis + 1]
        for axis in range(3)
    ]
    for axis in range(3):
        wave[axis] = jnp.broadcast_to(vectors[axis], (8, width))
    wave[3] = jnp.broadcast_to(
        vectors[0] * vectors[0] + vectors[1] * vectors[1] + vectors[2] * vectors[2], (8, width)
    )

    nproj, natom, ntype = proj_atom_ref.shape[1], atom_type_ref.shape[1], widths_ref.shape[1]
    nrow = 4 * nproj
    atoms = lax.rem(lax.broadcasted_iota(jnp.int32, (4 * natom, nproj), 0), natom)
    atom_hot = (atoms == proj_atom_ref[...]).astype(F32).astype(BF16)
    row_of = lax.broadcasted_iota(jnp.int32, (nrow, nproj), 0) // 4
    row_hot = (row_of == lax.broadcasted_iota(jnp.int32, (nrow, nproj), 1)).astype(F32).astype(BF16)
    hot = dot_t(row_hot, atom_hot)
    types = lax.broadcasted_iota(jnp.int32, (8, natom), 0)
    of_type = (types == atom_type_ref[...]).astype(F32)
    by_type = dot_t(hot[:, 0:natom].astype(BF16), of_type.astype(BF16))
    type_hot[...] = by_type
    weight = by_type[:, 0:1] * dion_ref[0:1, 0:1]
    for value in range(1, ntype):
        weight = weight + by_type[:, value : value + 1] * dion_ref[0:1, value : value + 1]
    strength_ref[...] = jnp.broadcast_to(weight, (nrow, 128))
    is_value = lax.rem(lax.broadcasted_iota(jnp.int32, (nrow, 4 * natom), 0), 4) == 0
    in_cos = lax.broadcasted_iota(jnp.int32, (nrow, 4 * natom), 1) < 2 * natom
    zero = jnp.zeros_like(hot)
    pick_cos[...] = jnp.where(is_value == in_cos, hot, zero).astype(BF16)
    pick_sin[...] = jnp.where(is_value, jnp.where(in_cos, zero, -hot), jnp.where(in_cos, hot, zero)).astype(
        BF16
    )

    centers = positions_ref[...].T
    row = lax.broadcasted_iota(jnp.int32, (8, LANES), 0)

    def tables(index, carry):
        columns = pl.ds(pl.multiple_of(index * LANES, LANES), LANES)
        k = [wave[axis, :, columns] for axis in range(4)]
        for first in range(0, natom, 16):
            parts = []
            for begin in (first, first + 8):
                place = centers[begin : begin + 8]
                parts.append(sin_cos(place[:, 0:1] * k[0] + place[:, 1:2] * k[1] + place[:, 2:3] * k[2]))
            for block, which in ((0, 1), (2, 0)):
                value = jnp.concatenate([parts[0][which], parts[1][which]], axis=0)
                upper = value.astype(BF16)
                waves[block * natom + first : block * natom + first + 16, columns] = upper
                waves[(block + 1) * natom + first : (block + 1) * natom + first + 16, columns] = (
                    value - upper.astype(F32)
                ).astype(BF16)
        kind = lax.rem(row, 4)
        along = jnp.where(kind == 1, k[0], jnp.where(kind == 2, k[1], k[2]))
        for value in range(ntype):
            spread = widths_ref[0:1, value : value + 1]
            envelope = jnp.exp(-0.5 * spread * k[3])
            for pair in range(2):
                channel = 2 * pair + row // 4
                if pair == 0:
                    angular = jnp.where(channel == 0, jnp.ones_like(along), k[0])
                else:
                    angular = jnp.where(channel == 2, k[1], k[2])
                matching = ((channel == kind) & (kind > 0)).astype(F32)
                factor = jnp.where(kind == 0, angular, matching - spread * along * angular)
                radial[value, 8 * pair : 8 * pair + 8, columns] = envelope * factor
        return carry

    lax.fori_loop(0, width // LANES, tables, 0)

    hrow = nrow // 2

    def build(half):
        rows = pl.ds(pl.multiple_of(half * hrow, hrow), hrow)
        left_cos, left_sin = pick_cos[rows, :], pick_sin[rows, :]
        kinds = type_hot[rows, :]

        def tile(index, carry):
            columns = pl.ds(pl.multiple_of(index * 256, 256), 256)
            right = waves[:, columns]
            table = [
                jnp.broadcast_to(radial[value, :, columns][None], (hrow // 16, 16, 256)).reshape(hrow, 256)
                for value in range(ntype)
            ]
            part = table[0]
            for value in range(1, ntype):
                part = jnp.where(kinds[:, value : value + 1] > 0.5, table[value], part)
            proj[0, rows, columns] = (part * jnp.dot(left_cos, right, preferred_element_type=F32)).astype(BF16)
            proj[1, rows, columns] = (part * jnp.dot(left_sin, right, preferred_element_type=F32)).astype(BF16)
            return carry

        lax.fori_loop(0, width // 256, tile, 0)

    build(1 - y_lo)
    for copy in loads[:2]:
        copy.wait()
    pl.semaphore_wait(barrier, nz - 1 + 2 * nband - 1)

    started = []

    def forward(src, block, count, bands):
        for band in bands:
            copy = put(src, occ_all.at[block], g_send.at[count], g_recv.at[block], p, band)
            copy.start()
            started.append(copy)
            count += 1
        return count

    def block_arrived(block):
        put(occ_all.at[block], occ_all.at[block], g_send.at[0], g_recv.at[block], p, b).wait_recv()

    mate_block = band_id(1 - y_hi, x, core)
    x_others = [(x + dx) % nx for dx in range(1, nx)]
    sent = forward(
        occ_all.at[b],
        b,
        0,
        [mate_block] + [band_id(y_hi, xx, core) for xx in x_others] + [band_id(y_hi, x, 1 - core)],
    )

    def project(half):
        rows = pl.ds(pl.multiple_of(half * hrow, hrow), hrow)
        real, imag = proj[0, rows, :], proj[1, rows, :]
        coef[0, rows, :] = dot_t(real, high_ref[0]) + dot_t(imag, high_ref[1])
        coef[1, rows, :] = dot_t(real, high_ref[1]) - dot_t(imag, high_ref[0])

    project(1 - y_lo)

    def chunk1(owner):
        return coef[:, pl.ds(pl.multiple_of(owner * 24, 8), 24), :].reshape(48, 256)

    def chunk2(owner):
        return total[:, :, pl.ds(pl.multiple_of(owner * 8, 8), 8), :].reshape(48, 256)

    def mate_sends(chunk, ys, yr, send, recv):
        copies = []
        for place, offset in enumerate(ORDER):
            ys[place] = chunk(pw_id(1 - y_lo, (z + offset + nz) % nz)).astype(BF16)
            copy = put(ys.at[place], yr.at[place], send.at[place], recv.at[place], y_mate, b)
            copy.start()
            copies.append(copy)
        return copies

    def reduce_z(chunk, mates, yr, zs, zr, send, recv, fill):
        copies = {}

        def local(offset):
            place = ORDER.index(offset)
            mates[place].wait_recv()
            return chunk(z_at(offset)) + yr[place].astype(F32)

        def push(slot, value, offset):
            zs[slot] = value.astype(BF16)
            copy = put(zs.at[slot], zr.at[slot], send.at[slot], recv.at[slot], z_at(offset), b)
            copy.start()
            copies[slot] = copy

        def arrived(slot):
            copies[slot].wait_recv()
            return zr[slot].astype(F32)

        for slot, (offset, target) in enumerate(MOVES):
            push(slot, local(offset), target if slot else 4 - 8 * odd)
        fill(0)
        relayed = [local(offset) for offset in RELAYS]
        for place, offset in enumerate(DIRECT):
            push(len(MOVES) + place, local(offset), offset)
        fill(1)
        farthest = arrived(0)
        for place, offset in enumerate(RELAYS):
            share = odd if place else 1 - odd
            value = relayed[place] + farthest * share.astype(F32)
            for slot, (_, target) in enumerate(MOVES):
                if slot and target * offset > 0:
                    value = value + arrived(slot)
            push(len(MOVES) + len(DIRECT) + place, value, offset)
        fill(2)
        value = local(0)
        for place in range(len(DIRECT) + len(RELAYS)):
            value = value + arrived(len(MOVES) + place)
        return value, list(copies.values())

    mates1 = mate_sends(chunk1, ys1, yr1, y1_send, y1_recv)
    build(y_lo)
    project(y_lo)
    block_arrived(mate_block)
    sent = forward(
        occ_all.at[mate_block],
        mate_block,
        sent,
        [band_id(y_hi, xx, core) for xx in x_others] + [band_id(y_hi, x, 1 - core)],
    )
    occ_a[...] = jnp.zeros_like(occ_a)
    occ_b[...] = jnp.zeros_like(occ_b)
    occ_a[0:nown, :] = occ_all[b, 0]
    occ_a[nown : 2 * nown, :] = occ_all[b, 1]
    occ_b[0:nown, :] = occ_all[b, 1]
    occ_b[nown : 2 * nown, :] = -occ_all[b, 0]
    occ_coef[...] = dot_t(proj[0], occ_a[...]) + dot_t(proj[1], occ_b[...])
    for owner in range(2 * nz):
        rows = occ_coef[24 * owner : 24 * owner + 24, :] * strength_ref[24 * owner : 24 * owner + 24, :]
        occ_tile[owner] = (
            rows[0:8] + pltpu.roll(rows[8:16], 32, 1) + pltpu.roll(rows[16:24], 64, 1)
        )
    def both_halves(dest):
        return jnp.concatenate([occ_tile[dest], occ_tile[nz + dest]], axis=0)

    spread_copies = []
    for step in range(1, nz):
        tile_send[step] = both_halves((z + step) % nz).astype(BF16)
        copy = put(
            tile_send.at[step], tile_recv.at[step], ts_send.at[step], ts_recv.at[step], z_at(step), b
        )
        copy.start()
        spread_copies.append(copy)

    nocc = total.shape[2]

    def momentum_piece(index):
        columns = pl.ds(pl.multiple_of(index * 256, 256), 256)
        for part in range(2):
            values = occ_all[:, part, :, columns].reshape(nocc, 256).astype(F32)
            for axis in range(3):
                vector = wave[axis, 0:1, columns]
                scaled[part, axis * nocc : (axis + 1) * nocc, :] = (values * vector).astype(BF16)
        real, imag = scaled[0], scaled[1]
        high_r, high_i = high_ref[0, :, columns], high_ref[1, :, columns]
        parts = (
            dot_t(real, high_r) + dot_t(imag, high_i),
            dot_t(real, high_i) - dot_t(imag, high_r),
        )
        for part in range(2):
            value = parts[part].reshape(3, nocc, 256)
            if index == 0:
                total[part] = value
            else:
                total[part] += value

    tile_copies = []

    def fill1(point):
        nonlocal sent
        if point == 0:
            for yy in (y_hi, 1 - y_hi):
                for xx in x_others:
                    block = band_id(yy, xx, core)
                    block_arrived(block)
                    sent = forward(occ_all.at[block], block, sent, [band_id(y_hi, x, 1 - core)])
        elif point == 1:
            for xx in [x] + x_others:
                for yy in range(2):
                    block_arrived(band_id(yy, xx, 1 - core))
            for index in range(3):
                momentum_piece(index)
        else:
            tile = both_halves(z)
            for copy, step in zip(spread_copies, range(1, nz)):
                copy.wait_recv()
                tile = tile + tile_recv[step].astype(F32)
            tile_own[0] = tile[0:8]
            tile_own[1] = tile[8:16]
            for step in range(nband):
                band = (b + step) % nband
                copy = put(
                    tile_own.at[1 - y_lo],
                    tiles.at[y_lo, b],
                    t_send.at[1, step],
                    t_recv.at[y_lo, b],
                    y_mate,
                    band,
                )
                copy.start()
                tile_copies.append(copy)
                if step:
                    copy = put(
                        tile_own.at[y_lo],
                        tiles.at[y_lo, b],
                        t_send.at[0, step],
                        t_recv.at[y_lo, b],
                        p,
                        band,
                    )
                    copy.start()
                    tile_copies.append(copy)
            tiles[y_lo, b] = tile_own[y_lo]
            for index in range(3, width // 256):
                momentum_piece(index)

    high_sum, moves1 = reduce_z(chunk1, mates1, yr1, zs1, zr1, z1_send, z1_recv, fill1)

    high_hi = high_sum.astype(BF16)
    high_lo = (high_sum - high_hi.astype(F32)).astype(BF16)
    rhs = jnp.concatenate([high_hi, high_lo, high_hi], axis=0)
    for step in range(nband):
        block = (b + step) % nband
        for side in ([y_lo, 1 - y_lo] if step else [1 - y_lo]):
            put(
                tile_own.at[0], tiles.at[side, block], t_send.at[0, 0], t_recv.at[side, block], p, b
            ).wait_recv()

    lane_block = lax.broadcasted_iota(jnp.int32, (8, 128), 1) // 16
    occ_sums = []
    for part in range(2):
        groups = []
        for group in range(3):
            halves = []
            for side in range(nband // 8):
                value = jnp.zeros((8, 128), F32)
                for place in range(8):
                    shift = (16 * place - 32 * group - 16 * part) % 128
                    tile = tiles[0, 8 * side + place] + tiles[1, 8 * side + place]
                    if shift:
                        tile = pltpu.roll(tile, shift, 1)
                    value = jnp.where(lane_block == place, tile, value)
                halves.append(value)
            groups.append(jnp.concatenate(halves, axis=1))
        occ_sums.append(jnp.concatenate(groups, axis=0))
    kind = lax.broadcasted_iota(jnp.int32, (24, 256), 0) % 4
    for axis in range(3):
        mixed = []
        for part in range(2):
            value = occ_sums[part]
            lower = pltpu.roll(value, axis + 1, 0)
            upper = pltpu.roll(value, 24 - (axis + 1), 0)
            mixed.append(
                jnp.where(kind == axis + 1, lower, jnp.where(kind == 0, -upper, jnp.zeros_like(value)))
            )
        for part in range(2):
            if part == 0:
                left = jnp.concatenate([mixed[1], -mixed[0]], axis=0)
            else:
                left = jnp.concatenate([mixed[0], mixed[1]], axis=0)
            left_hi = left.astype(BF16)
            left_lo = (left - left_hi.astype(F32)).astype(BF16)
            lhs = jnp.concatenate([left_hi, left_hi, left_lo], axis=0)
            lefts[3 * part + axis] = lhs

    def nonlocal_part(half):
        rows = pl.ds(pl.multiple_of(half * (nocc // 2), 128), nocc // 2)
        for part in range(2):
            for axis in range(3):
                total[part, axis, rows, :] += lax.dot_general(
                    lefts[3 * part + axis, :, rows], rhs, (((0,), (0,)), ((), ())), preferred_element_type=F32
                )

    nonlocal_part(1 - y_lo)
    mates2 = mate_sends(chunk2, ys2, yr2, y2_send, y2_recv)
    nonlocal_part(y_lo)
    result, moves2 = reduce_z(
        chunk2, mates2, yr2, zs2, zr2, z2_send, z2_recv, lambda point: None
    )
    result = result.reshape(2, 3, 8, 256)
    for axis in range(3):
        for part in range(2):
            out_ref[axis, part] = result[part, axis]

    for copy in (
        started + mates1 + spread_copies + moves1 + tile_copies + mates2 + moves2
    ):
        copy.wait_send()


def on_device(
    nz, nx, psi_occ, psi_high, miller, recip, kfrac, positions, atom_type, proj_atom, widths, dion
):
    nproj, natom, ntype = proj_atom.shape[0], positions.shape[0], widths.shape[0]
    nown, nhigh, width = psi_occ.shape[1], psi_high.shape[1], psi_high.shape[2]
    npw, nband = 2 * nz, 4 * nx
    nocc = nown * nband
    vmem = pltpu.VMEM
    dma = pltpu.SemaphoreType.DMA
    out = pl.pallas_call(
        functools.partial(kernel, nz, nx),
        out_shape=jax.ShapeDtypeStruct((3, 2, nocc // npw, nhigh), F32),
        in_specs=[pl.BlockSpec(memory_space=pltpu.HBM)] * 10,
        out_specs=pl.BlockSpec(memory_space=vmem),
        scratch_shapes=[
            vmem((2, nhigh, width), BF16),
            vmem((3, width), jnp.int32),
            vmem((3, 3), F32),
            vmem((1, 3), F32),
            vmem((3, natom), F32),
            vmem((1, natom), jnp.int32),
            vmem((1, nproj), jnp.int32),
            vmem((1, ntype), F32),
            vmem((1, ntype), F32),
            dma((10,)),
            vmem((nband, 2, nown, width), BF16),
            vmem((4, 8, width), F32),
            vmem((4 * natom, width), BF16),
            vmem((ntype, 16, width), F32),
            vmem((4 * nproj, 4 * natom), BF16),
            vmem((4 * nproj, 4 * natom), BF16),
            vmem((4 * nproj, 8), F32),
            vmem((4 * nproj, 128), F32),
            vmem((2, 4 * nproj, width), BF16),
            vmem((6, 144, nocc), BF16),
            vmem((128, width), BF16),
            vmem((128, width), BF16),
            vmem((2, 4 * nproj, nhigh), F32),
            vmem((4 * nproj, 128), F32),
            vmem((npw, 8, 128), F32),
            vmem((2, 3 * nocc, 256), BF16),
            vmem((2, 3, nocc, nhigh), F32),
            vmem((nz, 48, nhigh), BF16),
            vmem((nz, 48, nhigh), BF16),
            vmem((nz - 1, 48, nhigh), BF16),
            vmem((nz - 1, 48, nhigh), BF16),
            vmem((nz, 48, nhigh), BF16),
            vmem((nz, 48, nhigh), BF16),
            vmem((nz - 1, 48, nhigh), BF16),
            vmem((nz - 1, 48, nhigh), BF16),
            vmem((nz, 16, 128), BF16),
            vmem((nz, 16, 128), BF16),
            vmem((2, 8, 128), F32),
            vmem((2, nband, 8, 128), F32),
            dma((nband - 1,)),
            dma((nband,)),
            dma((nz,)),
            dma((nz,)),
            dma((nz,)),
            dma((nz,)),
            dma((nz - 1,)),
            dma((nz - 1,)),
            dma((nz,)),
            dma((nz,)),
            dma((nz - 1,)),
            dma((nz - 1,)),
            dma((2, nband)),
            dma((2, nband)),
        ],
        compiler_params=pltpu.CompilerParams(
            collective_id=0, has_side_effects=True, vmem_limit_bytes=64 * 1024 * 1024
        ),
    )(
        psi_occ,
        psi_high,
        miller,
        recip,
        kfrac[None],
        positions.T,
        atom_type[None],
        proj_atom[None],
        widths[None],
        dion[None],
    )
    return out


def solution(mesh):
    nz = mesh.shape["pw"] // 2
    nx = mesh.shape["band"] // 4
    placed = (
        P(None, "band", "pw"),
        P(None, "band", "pw"),
        P(None, "pw"),
        P(),
        P(),
        P(),
        P(),
        P(),
        P(),
        P(),
    )
    return jax.shard_map(
        functools.partial(on_device, nz, nx),
        mesh=mesh,
        in_specs=placed,
        out_specs=P(None, None, "pw", "band"),
        check_vma=False,
    )
```

```python
import functools

import jax
import jax.numpy as jnp
from jax import lax
from jax.experimental import pallas as pl
from jax.experimental.pallas import tpu as pltpu
from jax.sharding import PartitionSpec as P

MESH = pl.DeviceIdType.MESH
F32 = jnp.float32
BF16 = jnp.bfloat16
LANES = 512
MOVES = [(8, 4), (-7, -3), (7, 3), (-6, -2), (6, 2), (-5, -1), (5, 1)]
RELAYS = [4, -4]
DIRECT = [3, -3, 2, -2, 1, -1]
ORDER = [offset for offset, _ in MOVES] + RELAYS + DIRECT + [0]


def sin_cos(angle):
    turns = jnp.floor(angle * 0.6366197723675814 + 0.5)
    rest = angle - turns * 1.5703125
    rest = rest - turns * 4.837512969970703125e-4
    rest = rest - turns * 7.54978995489188216e-8
    square = rest * rest
    sine = rest + rest * square * (
        -1.6666654611e-1 + square * (8.3321608736e-3 + square * -1.9515295891e-4)
    )
    cosine = (
        1.0
        - 0.5 * square
        + square * square * (4.166664568298827e-2 + square * (-1.388731625493765e-3 + square * 2.443315711809948e-5))
    )
    quadrant = turns - 4.0 * jnp.floor(turns * 0.25)
    odd = (quadrant == 1.0) | (quadrant == 3.0)
    first = jnp.where(odd, cosine, sine)
    second = jnp.where(odd, sine, cosine)
    sine = jnp.where(quadrant >= 2.0, -first, first)
    cosine = jnp.where((quadrant == 1.0) | (quadrant == 2.0), -second, second)
    return sine, cosine


def dot_t(lhs, rhs):
    return lax.dot_general(lhs, rhs, (((1,), (1,)), ((), ())), preferred_element_type=F32)


def kernel(
    nz,
    nx,
    occ_hbm,
    high_hbm,
    miller_hbm,
    recip_hbm,
    kfrac_hbm,
    positions_hbm,
    atom_type_hbm,
    proj_atom_hbm,
    widths_hbm,
    dion_hbm,
    out_ref,
    high_ref,
    miller_ref,
    recip_ref,
    kfrac_ref,
    positions_ref,
    atom_type_ref,
    proj_atom_ref,
    widths_ref,
    dion_ref,
    in_sem,
    occ_all,
    wave,
    waves,
    radial,
    pick_cos,
    pick_sin,
    type_hot,
    strength_ref,
    proj,
    lefts,
    occ_a,
    occ_b,
    coef,
    occ_coef,
    occ_tile,
    scaled,
    total,
    ys1,
    yr1,
    zs1,
    zr1,
    ys2,
    yr2,
    zs2,
    zr2,
    tile_send,
    tile_recv,
    tile_own,
    tiles,
    g_send,
    g_recv,
    y1_send,
    y1_recv,
    ts_send,
    ts_recv,
    z1_send,
    z1_recv,
    y2_send,
    y2_recv,
    z2_send,
    z2_recv,
    t_send,
    t_recv,
):
    p = lax.axis_index("pw")
    b = lax.axis_index("band")
    nband = 4 * nx
    y_lo, z = p // nz, p % nz
    y_hi, x, core = b // (2 * nx), (b // 2) % nx, b % 2
    width, nown = high_hbm.shape[2], occ_hbm.shape[1]

    odd = z % 2

    def band_id(yy, xx, cc):
        return yy * (2 * nx) + xx * 2 + cc

    def pw_id(yy, zz):
        return yy * nz + zz

    def put(src, dst, send, recv, pw, band):
        return pltpu.make_async_remote_copy(
            src_ref=src,
            dst_ref=dst,
            send_sem=send,
            recv_sem=recv,
            device_id={"pw": pw, "band": band},
            device_id_type=MESH,
        )

    y_mate = pw_id(1 - y_lo, z)

    def z_at(offset):
        return pw_id(y_lo, (z + offset + nz) % nz)


    sources = (
        (occ_hbm, occ_all.at[b]),
        (high_hbm, high_ref),
        (miller_hbm, miller_ref),
        (recip_hbm, recip_ref),
        (kfrac_hbm, kfrac_ref),
        (positions_hbm, positions_ref),
        (atom_type_hbm, atom_type_ref),
        (proj_atom_hbm, proj_atom_ref),
        (widths_hbm, widths_ref),
        (dion_hbm, dion_ref),
    )
    loads = [
        pltpu.make_async_copy(src, dst, in_sem.at[place]) for place, (src, dst) in enumerate(sources)
    ]
    for copy in loads[2:] + loads[:2]:
        copy.start()
    barrier = pltpu.get_barrier_semaphore()
    for step in range(nband):
        pl.semaphore_signal(
            barrier, inc=1, device_id={"pw": y_mate, "band": (b + step) % nband}, device_id_type=MESH
        )
    for step in range(1, nz):
        pl.semaphore_signal(
            barrier, inc=1, device_id={"pw": z_at(step), "band": b}, device_id_type=MESH
        )
    for step in range(1, nband):
        pl.semaphore_signal(
            barrier, inc=1, device_id={"pw": p, "band": (b + step) % nband}, device_id_type=MESH
        )

    for copy in loads[2:]:
        copy.wait()
    shifted = [
        miller_ref[axis : axis + 1, :].astype(F32) + kfrac_ref[0:1, axis : axis + 1] for axis in range(3)
    ]
    vectors = [
        shifted[0] * recip_ref[0:1, axis : axis + 1]
        + shifted[1] * recip_ref[1:2, axis : axis + 1]
        + shifted[2] * recip_ref[2:3, axis : axis + 1]
        for axis in range(3)
    ]
    for axis in range(3):
        wave[axis] = jnp.broadcast_to(vectors[axis], (8, width))
    wave[3] = jnp.broadcast_to(
        vectors[0] * vectors[0] + vectors[1] * vectors[1] + vectors[2] * vectors[2], (8, width)
    )

    nproj, natom, ntype = proj_atom_ref.shape[1], atom_type_ref.shape[1], widths_ref.shape[1]
    nrow = 4 * nproj
    atoms = lax.rem(lax.broadcasted_iota(jnp.int32, (4 * natom, nproj), 0), natom)
    atom_hot = (atoms == proj_atom_ref[...]).astype(F32).astype(BF16)
    row_of = lax.broadcasted_iota(jnp.int32, (nrow, nproj), 0) // 4
    row_hot = (row_of == lax.broadcasted_iota(jnp.int32, (nrow, nproj), 1)).astype(F32).astype(BF16)
    hot = dot_t(row_hot, atom_hot)
    types = lax.broadcasted_iota(jnp.int32, (8, natom), 0)
    of_type = (types == atom_type_ref[...]).astype(F32)
    by_type = dot_t(hot[:, 0:natom].astype(BF16), of_type.astype(BF16))
    type_hot[...] = by_type
    weight = by_type[:, 0:1] * dion_ref[0:1, 0:1]
    for value in range(1, ntype):
        weight = weight + by_type[:, value : value + 1] * dion_ref[0:1, value : value + 1]
    strength_ref[...] = jnp.broadcast_to(weight, (nrow, 128))
    is_value = lax.rem(lax.broadcasted_iota(jnp.int32, (nrow, 4 * natom), 0), 4) == 0
    in_cos = lax.broadcasted_iota(jnp.int32, (nrow, 4 * natom), 1) < 2 * natom
    zero = jnp.zeros_like(hot)
    pick_cos[...] = jnp.where(is_value == in_cos, hot, zero).astype(BF16)
    pick_sin[...] = jnp.where(is_value, jnp.where(in_cos, zero, -hot), jnp.where(in_cos, hot, zero)).astype(
        BF16
    )

    centers = positions_ref[...].T
    row = lax.broadcasted_iota(jnp.int32, (8, LANES), 0)

    def tables(index, carry):
        columns = pl.ds(pl.multiple_of(index * LANES, LANES), LANES)
        k = [wave[axis, :, columns] for axis in range(4)]
        for first in range(0, natom, 16):
            parts = []
            for begin in (first, first + 8):
                place = centers[begin : begin + 8]
                parts.append(sin_cos(place[:, 0:1] * k[0] + place[:, 1:2] * k[1] + place[:, 2:3] * k[2]))
            for block, which in ((0, 1), (2, 0)):
                value = jnp.concatenate([parts[0][which], parts[1][which]], axis=0)
                upper = value.astype(BF16)
                waves[block * natom + first : block * natom + first + 16, columns] = upper
                waves[(block + 1) * natom + first : (block + 1) * natom + first + 16, columns] = (
                    value - upper.astype(F32)
                ).astype(BF16)
        kind = lax.rem(row, 4)
        along = jnp.where(kind == 1, k[0], jnp.where(kind == 2, k[1], k[2]))
        for value in range(ntype):
            spread = widths_ref[0:1, value : value + 1]
            envelope = jnp.exp(-0.5 * spread * k[3])
            for pair in range(2):
                channel = 2 * pair + row // 4
                if pair == 0:
                    angular = jnp.where(channel == 0, jnp.ones_like(along), k[0])
                else:
                    angular = jnp.where(channel == 2, k[1], k[2])
                matching = ((channel == kind) & (kind > 0)).astype(F32)
                factor = jnp.where(kind == 0, angular, matching - spread * along * angular)
                radial[value, 8 * pair : 8 * pair + 8, columns] = envelope * factor
        return carry

    lax.fori_loop(0, width // LANES, tables, 0)

    hrow = nrow // 2

    def build(half):
        rows = pl.ds(pl.multiple_of(half * hrow, hrow), hrow)
        left_cos, left_sin = pick_cos[rows, :], pick_sin[rows, :]
        kinds = type_hot[rows, :]

        def tile(index, carry):
            columns = pl.ds(pl.multiple_of(index * 256, 256), 256)
            right = waves[:, columns]
            table = [
                jnp.broadcast_to(radial[value, :, columns][None], (hrow // 16, 16, 256)).reshape(hrow, 256)
                for value in range(ntype)
            ]
            part = table[0]
            for value in range(1, ntype):
                part = jnp.where(kinds[:, value : value + 1] > 0.5, table[value], part)
            proj[0, rows, columns] = (part * jnp.dot(left_cos, right, preferred_element_type=F32)).astype(BF16)
            proj[1, rows, columns] = (part * jnp.dot(left_sin, right, preferred_element_type=F32)).astype(BF16)
            return carry

        lax.fori_loop(0, width // 256, tile, 0)

    build(1 - y_lo)
    for copy in loads[:2]:
        copy.wait()
    pl.semaphore_wait(barrier, nz - 1 + 2 * nband - 1)

    started = []

    def forward(src, block, count, bands):
        for band in bands:
            copy = put(src, occ_all.at[block], g_send.at[count], g_recv.at[block], p, band)
            copy.start()
            started.append(copy)
            count += 1
        return count

    def block_arrived(block):
        put(occ_all.at[block], occ_all.at[block], g_send.at[0], g_recv.at[block], p, b).wait_recv()

    mate_block = band_id(1 - y_hi, x, core)
    x_others = [(x + dx) % nx for dx in range(1, nx)]
    sent = forward(
        occ_all.at[b],
        b,
        0,
        [mate_block] + [band_id(y_hi, xx, core) for xx in x_others] + [band_id(y_hi, x, 1 - core)],
    )

    def project(half):
        rows = pl.ds(pl.multiple_of(half * hrow, hrow), hrow)
        real, imag = proj[0, rows, :], proj[1, rows, :]
        coef[0, rows, :] = dot_t(real, high_ref[0]) + dot_t(imag, high_ref[1])
        coef[1, rows, :] = dot_t(real, high_ref[1]) - dot_t(imag, high_ref[0])

    project(1 - y_lo)

    def chunk1(owner):
        return coef[:, pl.ds(pl.multiple_of(owner * 24, 8), 24), :].reshape(48, 256)

    def chunk2(owner):
        return total[:, :, pl.ds(pl.multiple_of(owner * 8, 8), 8), :].reshape(48, 256)

    def mate_sends(chunk, ys, yr, send, recv):
        copies = []
        for place, offset in enumerate(ORDER):
            ys[place] = chunk(pw_id(1 - y_lo, (z + offset + nz) % nz)).astype(BF16)
            copy = put(ys.at[place], yr.at[place], send.at[place], recv.at[place], y_mate, b)
            copy.start()
            copies.append(copy)
        return copies

    def reduce_z(chunk, mates, yr, zs, zr, send, recv, fill):
        copies = {}

        def local(offset):
            place = ORDER.index(offset)
            mates[place].wait_recv()
            return chunk(z_at(offset)) + yr[place].astype(F32)

        def push(slot, value, offset):
            zs[slot] = value.astype(BF16)
            copy = put(zs.at[slot], zr.at[slot], send.at[slot], recv.at[slot], z_at(offset), b)
            copy.start()
            copies[slot] = copy

        def arrived(slot):
            copies[slot].wait_recv()
            return zr[slot].astype(F32)

        for slot, (offset, target) in enumerate(MOVES):
            push(slot, local(offset), target if slot else 4 - 8 * odd)
        fill(0)
        relayed = [local(offset) for offset in RELAYS]
        for place, offset in enumerate(DIRECT):
            push(len(MOVES) + place, local(offset), offset)
        fill(1)
        farthest = arrived(0)
        for place, offset in enumerate(RELAYS):
            share = odd if place else 1 - odd
            value = relayed[place] + farthest * share.astype(F32)
            for slot, (_, target) in enumerate(MOVES):
                if slot and target * offset > 0:
                    value = value + arrived(slot)
            push(len(MOVES) + len(DIRECT) + place, value, offset)
        fill(2)
        value = local(0)
        for place in range(len(DIRECT) + len(RELAYS)):
            value = value + arrived(len(MOVES) + place)
        return value, list(copies.values())

    mates1 = mate_sends(chunk1, ys1, yr1, y1_send, y1_recv)
    build(y_lo)
    project(y_lo)
    block_arrived(mate_block)
    sent = forward(
        occ_all.at[mate_block],
        mate_block,
        sent,
        [band_id(y_hi, xx, core) for xx in x_others] + [band_id(y_hi, x, 1 - core)],
    )
    occ_a[...] = jnp.zeros_like(occ_a)
    occ_b[...] = jnp.zeros_like(occ_b)
    occ_a[0:nown, :] = occ_all[b, 0]
    occ_a[nown : 2 * nown, :] = occ_all[b, 1]
    occ_b[0:nown, :] = occ_all[b, 1]
    occ_b[nown : 2 * nown, :] = -occ_all[b, 0]
    occ_coef[...] = dot_t(proj[0], occ_a[...]) + dot_t(proj[1], occ_b[...])
    for owner in range(2 * nz):
        rows = occ_coef[24 * owner : 24 * owner + 24, :] * strength_ref[24 * owner : 24 * owner + 24, :]
        occ_tile[owner] = (
            rows[0:8] + pltpu.roll(rows[8:16], 32, 1) + pltpu.roll(rows[16:24], 64, 1)
        )
    def both_halves(dest):
        return jnp.concatenate([occ_tile[dest], occ_tile[nz + dest]], axis=0)

    spread_copies = []
    for step in range(1, nz):
        tile_send[step] = both_halves((z + step) % nz).astype(BF16)
        copy = put(
            tile_send.at[step], tile_recv.at[step], ts_send.at[step], ts_recv.at[step], z_at(step), b
        )
        copy.start()
        spread_copies.append(copy)

    nocc = total.shape[2]

    def momentum_piece(index):
        columns = pl.ds(pl.multiple_of(index * 256, 256), 256)
        for part in range(2):
            values = occ_all[:, part, :, columns].reshape(nocc, 256).astype(F32)
            for axis in range(3):
                vector = wave[axis, 0:1, columns]
                scaled[part, axis * nocc : (axis + 1) * nocc, :] = (values * vector).astype(BF16)
        real, imag = scaled[0], scaled[1]
        high_r, high_i = high_ref[0, :, columns], high_ref[1, :, columns]
        parts = (
            dot_t(real, high_r) + dot_t(imag, high_i),
            dot_t(real, high_i) - dot_t(imag, high_r),
        )
        for part in range(2):
            value = parts[part].reshape(3, nocc, 256)
            if index == 0:
                total[part] = value
            else:
                total[part] += value

    tile_copies = []

    def fill1(point):
        nonlocal sent
        if point == 0:
            for yy in (y_hi, 1 - y_hi):
                for xx in x_others:
                    block = band_id(yy, xx, core)
                    block_arrived(block)
                    sent = forward(occ_all.at[block], block, sent, [band_id(y_hi, x, 1 - core)])
        elif point == 1:
            for xx in [x] + x_others:
                for yy in range(2):
                    block_arrived(band_id(yy, xx, 1 - core))
            for index in range(3):
                momentum_piece(index)
            tile = both_halves(z)
            for copy, step in zip(spread_copies, range(1, nz)):
                copy.wait_recv()
                tile = tile + tile_recv[step].astype(F32)
            tile_own[0] = tile[0:8]
            tile_own[1] = tile[8:16]
            for step in range(nband):
                band = (b + step) % nband
                copy = put(
                    tile_own.at[1 - y_lo],
                    tiles.at[y_lo, b],
                    t_send.at[1, step],
                    t_recv.at[y_lo, b],
                    y_mate,
                    band,
                )
                copy.start()
                tile_copies.append(copy)
                if step:
                    copy = put(
                        tile_own.at[y_lo],
                        tiles.at[y_lo, b],
                        t_send.at[0, step],
                        t_recv.at[y_lo, b],
                        p,
                        band,
                    )
                    copy.start()
                    tile_copies.append(copy)
            tiles[y_lo, b] = tile_own[y_lo]
        else:
            for index in range(3, width // 256):
                momentum_piece(index)

    high_sum, moves1 = reduce_z(chunk1, mates1, yr1, zs1, zr1, z1_send, z1_recv, fill1)

    high_hi = high_sum.astype(BF16)
    high_lo = (high_sum - high_hi.astype(F32)).astype(BF16)
    rhs = jnp.concatenate([high_hi, high_lo, high_hi], axis=0)
    for step in range(nband):
        block = (b + step) % nband
        for side in ([y_lo, 1 - y_lo] if step else [1 - y_lo]):
            put(
                tile_own.at[0], tiles.at[side, block], t_send.at[0, 0], t_recv.at[side, block], p, b
            ).wait_recv()

    lane_block = lax.broadcasted_iota(jnp.int32, (8, 128), 1) // 16
    occ_sums = []
    for part in range(2):
        groups = []
        for group in range(3):
            halves = []
            for side in range(nband // 8):
                value = jnp.zeros((8, 128), F32)
                for place in range(8):
                    shift = (16 * place - 32 * group - 16 * part) % 128
                    tile = tiles[0, 8 * side + place] + tiles[1, 8 * side + place]
                    if shift:
                        tile = pltpu.roll(tile, shift, 1)
                    value = jnp.where(lane_block == place, tile, value)
                halves.append(value)
            groups.append(jnp.concatenate(halves, axis=1))
        occ_sums.append(jnp.concatenate(groups, axis=0))
    kind = lax.broadcasted_iota(jnp.int32, (24, 256), 0) % 4
    for axis in range(3):
        mixed = []
        for part in range(2):
            value = occ_sums[part]
            lower = pltpu.roll(value, axis + 1, 0)
            upper = pltpu.roll(value, 24 - (axis + 1), 0)
            mixed.append(
                jnp.where(kind == axis + 1, lower, jnp.where(kind == 0, -upper, jnp.zeros_like(value)))
            )
        for part in range(2):
            if part == 0:
                left = jnp.concatenate([mixed[1], -mixed[0]], axis=0)
            else:
                left = jnp.concatenate([mixed[0], mixed[1]], axis=0)
            left_hi = left.astype(BF16)
            left_lo = (left - left_hi.astype(F32)).astype(BF16)
            lhs = jnp.concatenate([left_hi, left_hi, left_lo], axis=0)
            lefts[3 * part + axis] = lhs

    def nonlocal_part(half):
        rows = pl.ds(pl.multiple_of(half * (nocc // 2), 128), nocc // 2)
        for part in range(2):
            for axis in range(3):
                total[part, axis, rows, :] += lax.dot_general(
                    lefts[3 * part + axis, :, rows], rhs, (((0,), (0,)), ((), ())), preferred_element_type=F32
                )

    nonlocal_part(1 - y_lo)
    mates2 = mate_sends(chunk2, ys2, yr2, y2_send, y2_recv)
    nonlocal_part(y_lo)
    result, moves2 = reduce_z(
        chunk2, mates2, yr2, zs2, zr2, z2_send, z2_recv, lambda point: None
    )
    result = result.reshape(2, 3, 8, 256)
    for axis in range(3):
        for part in range(2):
            out_ref[axis, part] = result[part, axis]

    for copy in (
        started + mates1 + spread_copies + moves1 + tile_copies + mates2 + moves2
    ):
        copy.wait_send()


def on_device(
    nz, nx, psi_occ, psi_high, miller, recip, kfrac, positions, atom_type, proj_atom, widths, dion
):
    nproj, natom, ntype = proj_atom.shape[0], positions.shape[0], widths.shape[0]
    nown, nhigh, width = psi_occ.shape[1], psi_high.shape[1], psi_high.shape[2]
    npw, nband = 2 * nz, 4 * nx
    nocc = nown * nband
    vmem = pltpu.VMEM
    dma = pltpu.SemaphoreType.DMA
    out = pl.pallas_call(
        functools.partial(kernel, nz, nx),
        out_shape=jax.ShapeDtypeStruct((3, 2, nocc // npw, nhigh), F32),
        in_specs=[pl.BlockSpec(memory_space=pltpu.HBM)] * 10,
        out_specs=pl.BlockSpec(memory_space=vmem),
        scratch_shapes=[
            vmem((2, nhigh, width), BF16),
            vmem((3, width), jnp.int32),
            vmem((3, 3), F32),
            vmem((1, 3), F32),
            vmem((3, natom), F32),
            vmem((1, natom), jnp.int32),
            vmem((1, nproj), jnp.int32),
            vmem((1, ntype), F32),
            vmem((1, ntype), F32),
            dma((10,)),
            vmem((nband, 2, nown, width), BF16),
            vmem((4, 8, width), F32),
            vmem((4 * natom, width), BF16),
            vmem((ntype, 16, width), F32),
            vmem((4 * nproj, 4 * natom), BF16),
            vmem((4 * nproj, 4 * natom), BF16),
            vmem((4 * nproj, 8), F32),
            vmem((4 * nproj, 128), F32),
            vmem((2, 4 * nproj, width), BF16),
            vmem((6, 144, nocc), BF16),
            vmem((128, width), BF16),
            vmem((128, width), BF16),
            vmem((2, 4 * nproj, nhigh), F32),
            vmem((4 * nproj, 128), F32),
            vmem((npw, 8, 128), F32),
            vmem((2, 3 * nocc, 256), BF16),
            vmem((2, 3, nocc, nhigh), F32),
            vmem((nz, 48, nhigh), BF16),
            vmem((nz, 48, nhigh), BF16),
            vmem((nz - 1, 48, nhigh), BF16),
            vmem((nz - 1, 48, nhigh), BF16),
            vmem((nz, 48, nhigh), BF16),
            vmem((nz, 48, nhigh), BF16),
            vmem((nz - 1, 48, nhigh), BF16),
            vmem((nz - 1, 48, nhigh), BF16),
            vmem((nz, 16, 128), BF16),
            vmem((nz, 16, 128), BF16),
            vmem((2, 8, 128), F32),
            vmem((2, nband, 8, 128), F32),
            dma((nband - 1,)),
            dma((nband,)),
            dma((nz,)),
            dma((nz,)),
            dma((nz,)),
            dma((nz,)),
            dma((nz - 1,)),
            dma((nz - 1,)),
            dma((nz,)),
            dma((nz,)),
            dma((nz - 1,)),
            dma((nz - 1,)),
            dma((2, nband)),
            dma((2, nband)),
        ],
        compiler_params=pltpu.CompilerParams(
            collective_id=0, has_side_effects=True, vmem_limit_bytes=64 * 1024 * 1024
        ),
    )(
        psi_occ,
        psi_high,
        miller,
        recip,
        kfrac[None],
        positions.T,
        atom_type[None],
        proj_atom[None],
        widths[None],
        dion[None],
    )
    return out


def solution(mesh):
    nz = mesh.shape["pw"] // 2
    nx = mesh.shape["band"] // 4
    placed = (
        P(None, "band", "pw"),
        P(None, "band", "pw"),
        P(None, "pw"),
        P(),
        P(),
        P(),
        P(),
        P(),
        P(),
        P(),
    )
    return jax.shard_map(
        functools.partial(on_device, nz, nx),
        mesh=mesh,
        in_specs=placed,
        out_specs=P(None, None, "pw", "band"),
        check_vma=False,
    )
```
